512 devices in a mesh: wide: 128 (over z, y, core), narrow: 4 (over x).
Axes of the slice: x: 4, y: 4, z: 16, core: 2. Of those that a mesh axis runs over, the one named last changes fastest.
Arguments:
- level_rhs: float32 [128, 1024, 512], P('wide', 'narrow'), may hold values from -6 to 6
- galerkin_cols: int32 [7, 128, 16, 5], P(None, 'wide', 'narrow'), may hold values from 0 to 5, as said below
- galerkin_blocks: bfloat16 [7, 128, 16, 5, 64, 64], P(None, 'wide', 'narrow'), as said below
- restrict_cols: int32 [7, 128, 16, 3], P(None, 'wide', 'narrow'), may hold values from 0 to 7, as said below
- restrict_blocks: bfloat16 [7, 128, 16, 3, 64, 64], P(None, 'wide', 'narrow'), as said below
- prolong_cols: int32 [7, 128, 16, 2], P(None, 'wide', 'narrow'), may hold values from 0 to 3, as said below
- prolong_blocks: bfloat16 [7, 128, 16, 2, 64, 64], P(None, 'wide', 'narrow'), as said below
- coarse_inverse: bfloat16 [1024, 1024], P('narrow'), may hold values from -1.5 to 1.5
Outputs:
- correction: float32 [128, 1024, 512], P('wide', 'narrow')
The draws below stay inside these ranges and needn't reach their ends.
Inputs may be any that keep to these rules, and one draw needn't show every extreme that they name: `galerkin_cols`: slot 0 of every block row names the row's own block; values below 4 name blocks of the same piece, 4 the last block of the piece before, 5 the first block of the piece after. At level k the entries of the 2**k subdomains of a group are equal. `galerkin_blocks`: at level k the blocks of the 2**k subdomains of a group are equal. The diagonal entries of every slot-0 block lie between 1 and 4. `restrict_cols`: values below 4 name blocks of the lower joined group, the others block value - 4 of the upper one; slots 0 and 1 of coarse block c name c and 4 + c. At level k the entries of the 2**(k+1) subdomains of a coarse group are equal. `restrict_blocks`: at level k the blocks of the 2**(k+1) subdomains of a coarse group are equal. `prolong_cols`: slot 0 names the fine block's own index. At level k the entries of the 2**k subdomains of a group are equal. `prolong_blocks`: at level k the blocks of the 2**k subdomains of a group are equal.
All inputs are finite; a program needn't handle non-finite values.
Results may differ from the reference program's by a relative error of at most 0.035.
Values may be sent and summed in bfloat16 or wider, within the bound.
A program may use at most 64 MiB of HBM per device.

```python
import math
import jax
import jax.numpy as jnp
from jax import lax

BS = 64
NB = 4
NNZ = 5
NNZ_R = 3
NNZ_P = 2
NRHS = 512
LEVELS = 7
SUBDOMAINS = 128
GROUP_ROWS = 16
N_NARROW = 4


def spread_levels(key, extra_shift, make_level):
    per_level = []
    for level_idx in range(LEVELS):
        stride = 2 ** (level_idx + extra_shift)
        base_draw = make_level(jax.random.fold_in(key, level_idx), SUBDOMAINS // stride)
        per_level.append(jnp.repeat(base_draw, stride, axis=0))
    return jnp.stack(per_level)


def row_blocks():
    return (jnp.arange(GROUP_ROWS, dtype=jnp.int32) % NB)[None, :, None]


def mixed_normal(sub_key, shape, scale):
    values = jax.random.normal(sub_key, shape, jnp.float32) * scale
    return values


def draw_galerkin_cols(key, part):

    def make_level(sub_key, group_count):
        random_ids = jax.random.randint(sub_key, (group_count, GROUP_ROWS, NNZ), 0, NB + 2, dtype=jnp.int32)
        slot_ids = jnp.arange(NNZ, dtype=jnp.int32)[None, None, :]
        own_block = row_blocks()
        chosen = jnp.where(slot_ids == 0, own_block, random_ids)
        chosen = jnp.where((slot_ids == 1) & (own_block == 0), NB, chosen)
        chosen = jnp.where((slot_ids == 2) & (own_block == NB - 1), NB + 1, chosen)
        return chosen.astype(jnp.int32)
    return spread_levels(key, 0, make_level)


def draw_galerkin_blocks(key, part):

    def make_level(sub_key, group_count):
        coupling = mixed_normal(jax.random.fold_in(sub_key, 1), (group_count, GROUP_ROWS, NNZ, BS, BS), 0.08)
        pivots = jnp.exp(jax.random.uniform(jax.random.fold_in(sub_key, 2), (group_count, GROUP_ROWS, BS), jnp.float32, 0.0, math.log(4.0)))
        on_diag = (jnp.arange(NNZ) == 0)[:, None, None] & jnp.eye(BS, dtype=bool)[None, :, :]
        result = jnp.where(on_diag[None, None], pivots[:, :, None, :, None], coupling)
        return result.astype(jnp.bfloat16)
    return spread_levels(key, 0, make_level)


def draw_restrict_cols(key, part):

    def make_level(sub_key, group_count):
        random_ids = jax.random.randint(sub_key, (group_count, GROUP_ROWS, NNZ_R), 0, 2 * NB, dtype=jnp.int32)
        slot_ids = jnp.arange(NNZ_R, dtype=jnp.int32)[None, None, :]
        own_block = row_blocks()
        chosen = jnp.where(slot_ids == 0, own_block, random_ids)
        chosen = jnp.where(slot_ids == 1, own_block + NB, chosen)
        return chosen.astype(jnp.int32)
    return spread_levels(key, 1, make_level)


def draw_restrict_blocks(key, part):

    def make_level(sub_key, group_count):
        result = mixed_normal(sub_key, (group_count, GROUP_ROWS, NNZ_R, BS, BS), 1.55 / math.sqrt(NNZ_R * BS))
        return result.astype(jnp.bfloat16)
    return spread_levels(key, 1, make_level)


def draw_prolong_cols(key, part):

    def make_level(sub_key, group_count):
        random_ids = jax.random.randint(sub_key, (group_count, GROUP_ROWS, NNZ_P), 0, NB, dtype=jnp.int32)
        slot_ids = jnp.arange(NNZ_P, dtype=jnp.int32)[None, None, :]
        chosen = jnp.where(slot_ids == 0, row_blocks(), random_ids)
        return chosen.astype(jnp.int32)
    return spread_levels(key, 0, make_level)


def draw_prolong_blocks(key, part):

    def make_level(sub_key, group_count):
        result = mixed_normal(sub_key, (group_count, GROUP_ROWS, NNZ_P, BS, BS), 1.5 / math.sqrt(NNZ_P * BS))
        return result.astype(jnp.bfloat16)
    return spread_levels(key, 0, make_level)


def steps_of(rng, shape, shards, low, largest):
    factor_of, own = 1.0, jax.random.fold_in(rng, 6)
    for position, shards_of in shards:
        heights = jnp.exp(jax.random.uniform(jax.random.fold_in(own, position), (shards_of,), jnp.float32, low / len(shards), largest / len(shards)))
        factor_of = factor_of * jnp.repeat(heights, shape[position] // shards_of).reshape([-1 if axis == position else 1 for axis in range(len(shape))])
    return factor_of


def gaussian(key, dims, spread, most, cuts=(), held_as=jnp.bfloat16):
    entries = jax.random.normal(key, dims, jnp.float32) * spread
    if len(cuts) > 0:
        entries = steps_of(key, dims, cuts, -0.22, 0.18) * entries
    return jnp.clip(entries, min=-most, max=most).astype(held_as)


def setup_inputs(seed: int = 0) -> dict:
    seeds = jax.random.split(jax.random.key(seed), 9)
    return {
        "level_rhs": gaussian(seeds[0], (SUBDOMAINS, GROUP_ROWS * BS, NRHS), 1.0, 6.0, ((0, 128), (1, 4)), jnp.float32),
        "galerkin_cols": draw_galerkin_cols(jax.random.fold_in(seeds[8], 71), 0),
        "galerkin_blocks": draw_galerkin_blocks(jax.random.fold_in(seeds[8], 71), 0),
        "restrict_cols": draw_restrict_cols(jax.random.fold_in(seeds[8], 71), 0),
        "restrict_blocks": draw_restrict_blocks(jax.random.fold_in(seeds[8], 71), 0),
        "prolong_cols": draw_prolong_cols(jax.random.fold_in(seeds[8], 71), 0),
        "prolong_blocks": draw_prolong_blocks(jax.random.fold_in(seeds[8], 71), 0),
        "coarse_inverse": gaussian(seeds[7], (GROUP_ROWS * BS, GROUP_ROWS * BS), (GROUP_ROWS * BS // 64) ** -0.5, 1.5, ((0, 4),)),
    }


relax_down = 0.7
relax_up = 0.5


def rim_extend(pieces, with_rims):
    zero_block = jnp.zeros((1, 1) + pieces.shape[2:], pieces.dtype)
    if with_rims:
        before = jnp.concatenate([zero_block, pieces[:-1, -1:]], axis=0)
        after = jnp.concatenate([pieces[1:, :1], zero_block], axis=0)
    else:
        before = jnp.zeros_like(pieces[:, :1])
        after = jnp.zeros_like(pieces[:, :1])
    return jnp.concatenate([pieces, before, after], axis=1)


def pick_piece(source_piece, piece_ids):
    return source_piece[piece_ids]


def take_blocks(source, col_ids):
    return jax.vmap(pick_piece)(source, col_ids)


def block_sum(blocks, picked):
    return jnp.einsum("jbsrc,jbscn->jbrn", blocks.astype(jnp.float32), picked.astype(jnp.float32), precision=lax.Precision.HIGHEST)


def apply_rims(operands):
    col_ids, blocks, rounded = operands
    return block_sum(blocks, take_blocks(rim_extend(rounded, True), col_ids))


def apply_local(operands):
    col_ids, blocks, rounded = operands
    return block_sum(blocks, take_blocks(rim_extend(rounded, False), col_ids))


def transfer(operands):
    col_ids, blocks, source = operands
    return block_sum(blocks, take_blocks(source, col_ids))


def reference(level_rhs, galerkin_cols, galerkin_blocks, restrict_cols, restrict_blocks, prolong_cols, prolong_blocks, coarse_inverse):
    current = level_rhs.reshape(SUBDOMAINS, N_NARROW, NB, BS, NRHS)
    stored = []
    for level_idx in range(LEVELS):
        stride = 2 ** level_idx
        groups = SUBDOMAINS // stride
        col_ids = galerkin_cols[level_idx, ::stride].reshape(groups, N_NARROW, NB, NNZ)
        blocks = galerkin_blocks[level_idx, ::stride].reshape(groups, N_NARROW, NB, NNZ, BS, BS)
        diagonal = jnp.diagonal(blocks[:, :, :, 0], axis1=-2, axis2=-1).astype(jnp.float32)[..., None]
        smoothed = relax_down * current / diagonal
        applied = lax.map(apply_rims, (col_ids, blocks, smoothed.astype(jnp.bfloat16)))
        residual = (current - applied).astype(jnp.bfloat16)
        paired = residual.reshape(groups // 2, 2, N_NARROW, NB, BS, NRHS)
        union = jnp.concatenate([paired[:, 0], paired[:, 1]], axis=2)
        rest_ids = restrict_cols[level_idx, ::2 * stride].reshape(groups // 2, N_NARROW, NB, NNZ_R)
        rest_blocks = restrict_blocks[level_idx, ::2 * stride].reshape(groups // 2, N_NARROW, NB, NNZ_R, BS, BS)
        stored.append((current, smoothed, diagonal, col_ids, blocks))
        current = lax.map(transfer, (rest_ids, rest_blocks, union))
    flat_rhs = current.astype(jnp.bfloat16).reshape(GROUP_ROWS * BS, NRHS)
    solution = jnp.dot(coarse_inverse, flat_rhs, preferred_element_type=jnp.float32).reshape(1, N_NARROW, NB, BS, NRHS)
    for level_idx in reversed(range(LEVELS)):
        stride = 2 ** level_idx
        groups = SUBDOMAINS // stride
        fine_rhs, smoothed, diagonal, col_ids, blocks = stored[level_idx]
        coarse_bf = jnp.repeat(solution.astype(jnp.bfloat16), 2, axis=0)
        pro_ids = prolong_cols[level_idx, ::stride].reshape(groups, N_NARROW, NB, NNZ_P)
        pro_blocks = prolong_blocks[level_idx, ::stride].reshape(groups, N_NARROW, NB, NNZ_P, BS, BS)
        updated = smoothed + lax.map(transfer, (pro_ids, pro_blocks, coarse_bf))
        applied = lax.map(apply_local, (col_ids, blocks, updated.astype(jnp.bfloat16)))
        solution = updated + relax_up * (fine_rhs - applied) / diagonal
    return solution.reshape(SUBDOMAINS, GROUP_ROWS * BS, NRHS)
```

```python
import jax
import jax.numpy as jnp
from jax import lax
from jax.experimental import pallas as pl
from jax.experimental.pallas import tpu as pltpu
from jax.sharding import PartitionSpec as P

relax_down = 0.7
relax_up = 0.5

LEVELS = 7
BS = 64
NB = 4
ROWS = NB * BS
CH = 128
STD = 2
SPLIT = (True, True, True, True, False, False, False)

f32 = jnp.float32
bf16 = jnp.bfloat16
NT = (((1,), (1,)), ((), ()))


def dot_nn(a, b):
    return jnp.dot(a, b, preferred_element_type=f32)


def dot_nt(a, b):
    return lax.dot_general(a, b, NT, preferred_element_type=f32)


def field_counts():
    counts = [4 * CH]
    for level in range(LEVELS):
        counts.append(counts[-1] // 2 if SPLIT[level] else counts[-1])
    return counts


FIELDS = field_counts()


def kernel(
    gcol, rcol, pcol, rhs_hbm, a_hbm, r_hbm, p_hbm, inv_hbm, out_hbm,
    b0, a_raw, r_raw, p_raw, cinv,
    a_own, a_halo, r_own, r_oth, p_own, dcol, drow,
    s0, s1, h0, h1, acc0, acc1, u0, u1, ro0, ro1, b1,
    bt, st, hs, hr, rt, ut, g_send, g_recv, xt, xq, x2o, x1b, x1r, outv,
    load_sem, out_sem, send_sem, recv_sem,
):
    w = lax.axis_index("wide")
    j = lax.axis_index("narrow")
    nxt = lax.rem(j + 1, 4)
    prv = lax.rem(j + 3, 4)
    bits = [lax.rem(w // (1 << k), 2) for k in range(LEVELS)]
    partners = [w + (1 - 2 * bits[k]) * (1 << k) for k in range(LEVELS)]

    barrier = pltpu.get_barrier_semaphore()
    for d in (1, 2, 3):
        pl.semaphore_signal(barrier, inc=1, device_id={"narrow": lax.rem(j + d, 4)})
    for k in range(LEVELS):
        pl.semaphore_signal(barrier, inc=1, device_id={"wide": partners[k]})

    own_q = bits[0] * 2 + bits[1]
    oth_q = bits[0] * 2 + (1 - bits[1])
    par_q = (1 - bits[0]) * 2 + bits[1]
    par_o = (1 - bits[0]) * 2 + (1 - bits[1])
    chunk = [par_o, par_q, oth_q, own_q]

    def lanes(slot):
        return pl.ds(pl.multiple_of(chunk[slot] * CH, CH), CH)

    n_load = [0]

    def load(src, dst):
        copy = pltpu.make_async_copy(src, dst, load_sem.at[n_load[0]])
        n_load[0] += 1
        copy.start()
        return copy

    ld_b = [load(rhs_hbm.at[0, :, lanes(i)], b0.at[i]) for i in range(2)]
    ld_a = {0: load(a_hbm.at[0, 0], a_raw.at[0])}
    ld_b += [load(rhs_hbm.at[0, :, lanes(i)], b0.at[i]) for i in (2, 3)]
    ld_r = {0: load(r_hbm.at[0, 0], r_raw.at[0])}
    ld_a[1] = load(a_hbm.at[1, 0], a_raw.at[1])
    ld_r[1] = load(r_hbm.at[1, 0], r_raw.at[1])
    for k in range(2, LEVELS):
        ld_a[k] = load(a_hbm.at[k, 0], a_raw.at[k])
        ld_r[k] = load(r_hbm.at[k, 0], r_raw.at[k])
    ld_p = load(p_hbm.at[:, 0], p_raw)
    ld_i = load(inv_hbm, cinv)

    n_rem = [0]

    def remote(src, dst, axis, where):
        idx = n_rem[0]
        n_rem[0] += 1
        return pltpu.make_async_remote_copy(
            src_ref=src, dst_ref=dst, send_sem=send_sem.at[idx], recv_sem=recv_sem.at[idx],
            device_id={axis: where}, device_id_type=pl.DeviceIdType.MESH,
        )

    started = []

    def go(copy):
        copy.start()
        started.append(copy)
        return copy

    lane = lax.broadcasted_iota(jnp.int32, (BS, 2 * BS), 1)
    row = lax.broadcasted_iota(jnp.int32, (BS, 2 * BS), 0)
    upper = lane // BS
    lo_code = jnp.where(j > 0, NB, -1)
    hi_code = jnp.where(j < 3, NB + 1, -1)
    halo_lo = jnp.where(upper == 0, lo_code, -1)
    halo_hi = jnp.where(upper == 1, hi_code, -1)
    halo_both = jnp.where(upper == 0, lo_code, hi_code)

    def doubled(block):
        wide = block.astype(f32)
        return jnp.concatenate([wide, wide], axis=1)

    def pick(code, ids, blocks):
        total = jnp.where(code == ids[0], blocks[0], 0.0)
        for c, blk in zip(ids[1:], blocks[1:]):
            total = total + jnp.where(code == c, blk, 0.0)
        return total.astype(bf16)

    def prep_a(k):
        ld_a[k].wait()

        def body(b, carry):
            at = pl.ds(pl.multiple_of(b * BS, BS), BS)
            ids = [gcol[k, 0, b, s] for s in range(5)]
            blocks = [doubled(a_raw[k, b, s]) for s in range(5)]
            a_own[k, at, 0:128] = pick(upper, ids, blocks)
            a_own[k, at, 128:256] = pick(upper + 2, ids, blocks)
            if k < STD:
                a_halo[k, at, 0:128] = pick(halo_both, ids, blocks)
            else:
                a_halo[k, at, 0:128] = pick(halo_lo, ids, blocks)
                a_halo[k, at, 128:256] = pick(halo_hi, ids, blocks)
            return carry

        lax.fori_loop(0, NB, body, 0)
        if k >= STD:
            for p in range(2):
                lo = doubled(a_raw[k, 2 * p, 0])
                hi = doubled(a_raw[k, 2 * p + 1, 0])
                diag = jnp.where(row == lane, lo, 0.0) + jnp.where(row + BS == lane, hi, 0.0)
                drow[k, 0:1, p * 128:(p + 1) * 128] = 1.0 / jnp.sum(diag, axis=0, keepdims=True)

    def prep_dcol(k):
        def body(b, carry):
            at = pl.ds(pl.multiple_of(b * BS, BS), BS)
            blk = doubled(a_raw[k, b, 0])
            d = jnp.sum(jnp.where(row == lane, blk, 0.0), axis=1, keepdims=True)
            dcol[k, at, :] = jnp.broadcast_to(1.0 / d, (BS, CH))
            return carry

        lax.fori_loop(0, NB, body, 0)

    def prep_r(k):
        ld_r[k].wait()

        def body(b, carry):
            at = pl.ds(pl.multiple_of(b * BS, BS), BS)
            ids = [rcol[k, 0, b, s] for s in range(3)]
            blocks = [doubled(r_raw[k, b, s]) for s in range(3)]
            for p in range(2):
                sl = slice(p * 128, (p + 1) * 128)
                r_own[k, at, sl] = pick(upper + (2 * p + NB * bits[k]), ids, blocks)
                r_oth[k, at, sl] = pick(upper + (2 * p + NB * (1 - bits[k])), ids, blocks)
            return carry

        lax.fori_loop(0, NB, body, 0)

    def prep_p(k):
        def body(b, carry):
            at = pl.ds(pl.multiple_of(b * BS, BS), BS)
            ids = [pcol[k, 0, b, s] for s in range(2)]
            blocks = [doubled(p_raw[k, b, s]) for s in range(2)]
            for p in range(2):
                p_own[k, at, p * 128:(p + 1) * 128] = pick(upper + 2 * p, ids, blocks)
            return carry

        lax.fori_loop(0, NB, body, 0)

    ld_a[0].wait()
    ld_a[0] = type("Done", (), {"wait": lambda self: None})()
    prep_dcol(0)
    sends_h0 = []
    for pair in range(2):
        for i in (2 * pair, 2 * pair + 1):
            ld_b[i].wait()
            s0[i] = (relax_down * b0[i] * dcol[0]).astype(bf16)
        if pair == 0:
            pl.semaphore_wait(barrier, 3 + LEVELS)
        at = pl.ds(2 * pair, 2)
        sends_h0.append((
            go(remote(s0.at[at, 192:256], h0.at[at, 0:64], "narrow", nxt)),
            go(remote(s0.at[at, 0:64], h0.at[at, 64:128], "narrow", prv)),
        ))
    prep_a(0)
    for i in range(4):
        acc0[i] = b0[i] - dot_nn(a_own[0], s0[i])
    for copy in sends_h0[0]:
        copy.wait_recv()
    ex0 = []
    for i in range(2):
        ro0[i] = (acc0[i] - dot_nn(a_halo[0, :, 0:128], h0[i])).astype(bf16)
        ex0.append(go(remote(ro0.at[i], u0.at[i], "wide", partners[0])))
    for copy in sends_h0[1]:
        copy.wait_recv()
    for i in (2, 3):
        ro0[i] = (acc0[i] - dot_nn(a_halo[0, :, 0:128], h0[i])).astype(bf16)
    prep_r(0)
    for i in range(2):
        acc1[i] = dot_nn(r_own[0], ro0[2 + i])
    ld_a[1].wait()
    ld_a[1] = ld_a[0]
    prep_dcol(1)
    sends_h1 = []
    for i in range(2):
        ex0[i].wait_recv()
        b1[i] = acc1[i] + dot_nn(r_oth[0], u0[i])
        s1[i] = (relax_down * b1[i] * dcol[1]).astype(bf16)
        sends_h1.append((
            go(remote(s1.at[i, 192:256], h1.at[i, 0:64], "narrow", nxt)),
            go(remote(s1.at[i, 0:64], h1.at[i, 64:128], "narrow", prv)),
        ))
    prep_a(1)
    for i in range(2):
        acc1[i] = b1[i] - dot_nn(a_own[1], s1[i])
    for i in range(2):
        for copy in sends_h1[i]:
            copy.wait_recv()
        ro1[i] = (acc1[i] - dot_nn(a_halo[1, :, 0:128], h1[i])).astype(bf16)
        if i == 0:
            ex1 = go(remote(ro1.at[0], u1, "wide", partners[1]))
    prep_r(1)
    part = dot_nn(r_own[1], ro1[1])
    acc1[1] = part
    prep_a(2)
    ex1.wait_recv()
    current = jnp.transpose(acc1[1] + dot_nn(r_oth[1], u1[...]))

    for k in range(STD, LEVELS):
        t = k - STD
        n = FIELDS[k]
        m = FIELDS[k + 1]
        bt[t, 0:n, :] = current
        smooth = relax_down * current * drow[k, 0:1, :]
        s_bf = smooth.astype(bf16)
        turned0 = pltpu.roll(smooth[:, 0:128], BS, 1)
        turned1 = pltpu.roll(smooth[:, 128:256], BS, 1)
        lane_n = lax.broadcasted_iota(jnp.int32, (n, 128), 1)
        hs[t, 0:n, :] = jnp.where(lane_n < BS, turned1, turned0).astype(bf16)
        send_a = go(remote(hs.at[t, 0:n], hr.at[t, 0:n, 0:128], "narrow", nxt))
        send_b = go(remote(hs.at[t, 0:n], hr.at[t, 0:n, 128:256], "narrow", prv))
        rest = current - dot_nt(s_bf, a_own[k])
        st[t, 0:n, :] = rest
        prep_r(k)
        send_a.wait_recv()
        send_b.wait_recv()
        rt[t, 0:n, :] = (st[t, 0:n, :] - dot_nt(hr[t, 0:n, :], a_halo[k])).astype(bf16)
        if SPLIT[k]:
            keep = pl.ds(pl.multiple_of(bits[k] * m, m), m)
            give = pl.ds(pl.multiple_of((1 - bits[k]) * m, m), m)
        else:
            keep = give = pl.ds(0, m)
        ex = go(remote(rt.at[t, give], ut.at[t, 0:m], "wide", partners[k]))
        bt[t + 1, 0:m, :] = dot_nt(rt[t, keep, :], r_own[k])
        if k + 1 < LEVELS:
            prep_a(k + 1)
        else:
            ld_p.wait()
            prep_p(6)
            ld_i.wait()
        ex.wait_recv()
        current = bt[t + 1, 0:m, :] + dot_nt(ut[t, 0:m, :], r_oth[k])

    n = FIELDS[LEVELS]
    g_send[...] = current.astype(bf16)
    gathers = [
        go(remote(g_send, g_recv.at[d - 1], "narrow", lax.rem(j + 4 - d, 4))) for d in (1, 2, 3)
    ]

    def inverse_cols(d):
        return cinv[:, pl.ds(pl.multiple_of(lax.rem(j + d, 4) * ROWS, ROWS), ROWS)]

    bt[LEVELS - STD, 0:n, :] = dot_nt(g_send[...], inverse_cols(0))
    for k in reversed(range(LEVELS - 1)):
        prep_p(k)
    for copy in gathers:
        copy.wait_recv()
    current = bt[LEVELS - STD, 0:n, :]
    for d in (1, 2, 3):
        current = current + dot_nt(g_recv[d - 1], inverse_cols(d))

    def up_rows(k, rows, x_bf):
        t = k - STD
        rhs = bt[t, rows, :]
        dinv = drow[k, 0:1, :]
        y = relax_down * rhs * dinv + dot_nt(x_bf, p_own[k])
        applied = dot_nt(y.astype(bf16), a_own[k])
        return y + relax_up * (rhs - applied) * dinv

    for k in reversed(range(STD, LEVELS)):
        t = k - STD
        n, m = FIELDS[k], FIELDS[k + 1]
        if SPLIT[k]:
            keep = pl.ds(pl.multiple_of(bits[k] * m, m), m)
            give = pl.ds(pl.multiple_of((1 - bits[k]) * m, m), m)
            xt[t, keep, :] = current.astype(bf16)
            ex = go(remote(xt.at[t, keep], xt.at[t, keep], "wide", partners[k]))
            xq[t, keep, :] = up_rows(k, keep, xt[t, keep, :])
            ex.wait_recv()
            xq[t, give, :] = up_rows(k, give, xt[t, give, :])
            current = xq[t, 0:n, :]
        else:
            current = up_rows(k, slice(0, n), current.astype(bf16))

    xt[LEVELS - STD, 0:CH, :] = current.astype(bf16)
    ex_up1 = go(remote(xt.at[LEVELS - STD, 0:CH], x2o, "wide", partners[1]))

    def up_cols(rhs, dinv, prolonged, a):
        y = relax_down * rhs * dinv + prolonged
        applied = dot_nn(a, y.astype(bf16))
        return y + relax_up * (rhs - applied) * dinv

    x1b[1] = up_cols(b1[1], dcol[1], dot_nt(p_own[1], xt[LEVELS - STD, 0:CH, :]), a_own[1]).astype(bf16)
    ex_up0 = [None, go(remote(x1b.at[1], x1r.at[1], "wide", partners[0]))]
    outs = []

    def finish(slot, x_bf):
        outv[slot] = up_cols(b0[slot], dcol[0], dot_nn(p_own[0], x_bf), a_own[0])
        copy = pltpu.make_async_copy(outv.at[slot], out_hbm.at[0, :, lanes(slot)], out_sem.at[slot])
        copy.start()
        outs.append(copy)

    ex_up1.wait_recv()
    x1b[0] = up_cols(b1[0], dcol[1], dot_nt(p_own[1], x2o[...]), a_own[1]).astype(bf16)
    ex_up0[0] = go(remote(x1b.at[0], x1r.at[0], "wide", partners[0]))
    finish(3, x1b[1])
    finish(2, x1b[0])
    for i in (1, 0):
        ex_up0[i].wait_recv()
        finish(i, x1r[i])
    for copy in started:
        copy.wait_send()
    for copy in outs:
        copy.wait()


REMOTES = 44


def on_device(*args):
    rhs, gcol, galerkin, rcol, restrict, pcol, prolong, inverse = args
    deep = LEVELS - STD
    top = FIELDS[STD]
    last = FIELDS[LEVELS]
    vmem = pltpu.VMEM
    scratch = [
        vmem((4, ROWS, CH), f32),
        vmem((LEVELS, NB, 5, BS, BS), bf16),
        vmem((LEVELS, NB, 3, BS, BS), bf16),
        vmem((LEVELS, NB, 2, BS, BS), bf16),
        vmem((ROWS, 4 * ROWS), bf16),
        vmem((LEVELS, ROWS, ROWS), bf16),
        vmem((LEVELS, ROWS, ROWS), bf16),
        vmem((LEVELS, ROWS, ROWS), bf16),
        vmem((LEVELS, ROWS, ROWS), bf16),
        vmem((LEVELS, ROWS, ROWS), bf16),
        vmem((STD, ROWS, CH), f32),
        vmem((LEVELS, 8, ROWS), f32),
        vmem((4, ROWS, CH), bf16),
        vmem((2, ROWS, CH), bf16),
        vmem((4, 2 * BS, CH), bf16),
        vmem((2, 2 * BS, CH), bf16),
        vmem((4, ROWS, CH), f32),
        vmem((2, ROWS, CH), f32),
        vmem((2, ROWS, CH), bf16),
        vmem((ROWS, CH), bf16),
        vmem((4, ROWS, CH), bf16),
        vmem((2, ROWS, CH), bf16),
        vmem((2, ROWS, CH), f32),
        vmem((deep + 1, top, ROWS), f32),
        vmem((deep, top, ROWS), f32),
        vmem((deep, top, 128), bf16),
        vmem((deep, top, ROWS), bf16),
        vmem((deep, top, ROWS), bf16),
        vmem((deep, top, ROWS), bf16),
        vmem((last, ROWS), bf16),
        vmem((3, last, ROWS), bf16),
        vmem((deep + 1, top, ROWS), bf16),
        vmem((deep, top, ROWS), f32),
        vmem((CH, ROWS), bf16),
        vmem((2, ROWS, CH), bf16),
        vmem((2, ROWS, CH), bf16),
        vmem((4, ROWS, CH), f32),
        pltpu.SemaphoreType.DMA((32,)),
        pltpu.SemaphoreType.DMA((4,)),
        pltpu.SemaphoreType.DMA((REMOTES,)),
        pltpu.SemaphoreType.DMA((REMOTES,)),
    ]
    smem = pl.BlockSpec(memory_space=pltpu.SMEM)
    hbm = pl.BlockSpec(memory_space=pl.ANY)
    return pl.pallas_call(
        kernel,
        out_shape=jax.ShapeDtypeStruct(rhs.shape, f32),
        in_specs=[smem, smem, smem, hbm, hbm, hbm, hbm, hbm],
        out_specs=hbm,
        scratch_shapes=scratch,
        compiler_params=pltpu.CompilerParams(
            collective_id=0, has_side_effects=True, vmem_limit_bytes=60 * 1024 * 1024
        ),
    )(gcol, rcol, pcol, rhs, galerkin, restrict, prolong, inverse)


def solution(mesh):
    in_specs = (
        P("wide", "narrow", None),
        P(None, "wide", "narrow", None),
        P(None, "wide", "narrow", None, None, None),
        P(None, "wide", "narrow", None),
        P(None, "wide", "narrow", None, None, None),
        P(None, "wide", "narrow", None),
        P(None, "wide", "narrow", None, None, None),
        P("narrow", None),
    )
    out_specs = P("wide", "narrow", None)
    return jax.shard_map(
        on_device, mesh=mesh, in_specs=in_specs, out_specs=out_specs, check_vma=False
    )
```

```python
import jax
import jax.numpy as jnp
from jax import lax
from jax.experimental import pallas as pl
from jax.experimental.pallas import tpu as pltpu
from jax.sharding import PartitionSpec as P

relax_down = 0.7
relax_up = 0.5

LEVELS = 7
SPLITS = 4
BS = 64
NB = 4
ROWS = NB * BS
ALL = 512
PIECES = 4
REMOTES = 96

f32 = jnp.float32
bf16 = jnp.bfloat16
NT = (((1,), (1,)), ((), ()))
FIELDS = [ALL >> min(level, SPLITS) for level in range(LEVELS + 1)]


def dot_nn(a, b):
    return jnp.dot(a, b, preferred_element_type=f32)


def dot_nt(a, b):
    return lax.dot_general(a, b, NT, preferred_element_type=f32)


def scratch_specs():
    vmem, dma = pltpu.VMEM, pltpu.SemaphoreType.DMA
    specs = {
        "gcol": pltpu.SMEM((1, 5, NB, LEVELS), jnp.int32),
        "rcol": pltpu.SMEM((1, 3, NB, LEVELS), jnp.int32),
        "pcol": pltpu.SMEM((1, NB, 2, LEVELS), jnp.int32),
        "b_std": vmem((ROWS, ALL), f32),
        "a_raw": vmem((LEVELS, NB, 5, BS, BS), bf16),
        "r_raw": vmem((LEVELS, NB, 3, BS, BS), bf16),
        "p_raw": vmem((LEVELS, NB, 2, BS, BS), bf16),
        "cinv": vmem((ROWS, PIECES * ROWS), bf16),
        "a_cat": vmem((LEVELS, ROWS, 2 * ROWS), bf16),
        "r_own": vmem((ROWS, ROWS), bf16),
        "p_own": vmem((ROWS, ROWS), bf16),
        "tmat": vmem((LEVELS, ROWS + 128, 2 * ROWS), bf16),
        "mmat": vmem((LEVELS, ROWS, ROWS), bf16),
        "deep": vmem((ROWS, ROWS), bf16),
        "fine": vmem((ROWS, ROWS), bf16),
        "kmat": vmem((ROWS, PIECES * ROWS), bf16),
        "drow": vmem((LEVELS, 8, ROWS), f32),
        "dcol": vmem((LEVELS, ROWS, 128), f32),
        "dsend": vmem((LEVELS, 8, 128), f32),
        "dhalo": vmem((2, LEVELS, 8, 128), f32),
        "h_send": vmem((ALL, 128), bf16),
        "h_recv": vmem((2, ALL, 128), bf16),
        "ctot": vmem((FIELDS[LEVELS], ROWS), f32),
        "c_std": vmem((ROWS, ALL), f32),
        "b7": vmem((PIECES, FIELDS[LEVELS], ROWS), bf16),
        "xg": vmem((ALL, ROWS), bf16),
        "outv": vmem((ROWS, ALL), f32),
        "load_sem": dma((32,)),
        "out_sem": dma((4,)),
        "send_sem": dma((REMOTES,)),
        "recv_sem": dma((REMOTES,)),
    }
    for k in range(LEVELS):
        n, m = FIELDS[k], FIELDS[k + 1]
        specs[f"bcat{k}"] = vmem((n, 2 * ROWS), bf16)
        specs[f"b32_{k + 1}"] = vmem((m, ROWS), f32)
        specs[f"pown{k}"] = vmem((m, ROWS), f32)
        specs[f"psend{k}"] = vmem((m, ROWS), bf16)
        specs[f"precv{k}"] = vmem((m, ROWS), bf16)
        if k < LEVELS - 1:
            specs[f"egive{k}"] = vmem((m, 128), bf16)
            specs[f"ekeep{k}"] = vmem((m, 128), bf16)
            specs[f"erecv{k}"] = vmem((4, m, 128), bf16)
        if 1 <= k < SPLITS:
            specs[f"cfull{k}"] = vmem((ALL, ROWS), bf16)
    return specs


class Refs:
    pass


def kernel(gcol_hbm, rcol_hbm, pcol_hbm, rhs_hbm, a_hbm, r_hbm, p_hbm, inv_hbm, out_hbm, *refs):
    v = Refs()
    for name, ref in zip(scratch_specs(), refs):
        setattr(v, name, ref)
    w = lax.axis_index("wide")
    j = lax.axis_index("narrow")
    nxt = lax.rem(j + 1, PIECES)
    prv = lax.rem(j + PIECES - 1, PIECES)
    has_next = j < PIECES - 1
    has_prev = j > 0
    bits = [lax.rem(w // (1 << k), 2) for k in range(LEVELS)]

    def across(mask):
        other = w
        for k in range(LEVELS):
            if mask >> k & 1:
                other = other + (1 - 2 * bits[k]) * (1 << k)
        return other

    partners = [across(1 << k) for k in range(LEVELS)]
    mates = range(1, 1 << SPLITS)

    barrier = pltpu.get_barrier_semaphore()
    greeted = [{"narrow": lax.rem(j + d, PIECES)} for d in (1, 2, 3)]
    greeted += [{"wide": p} for p in partners]
    greeted += [{"wide": p, "narrow": q} for p in partners[:-1] for q in (nxt, prv)]
    greeted += [{"wide": across(mask)} for mask in mates if mask & (mask - 1)]
    for where in greeted:
        pl.semaphore_signal(barrier, inc=1, device_id=where)

    n_load = [0]

    def load(src, dst):
        copy = pltpu.make_async_copy(src, dst, v.load_sem.at[n_load[0]])
        n_load[0] += 1
        copy.start()
        return copy

    ld_b = load(rhs_hbm.at[0], v.b_std)
    ld_g = load(gcol_hbm, v.gcol)
    ld_rc = load(rcol_hbm, v.rcol)
    ld_pc = load(pcol_hbm, v.pcol)
    ld_a0 = load(a_hbm.at[0, 0], v.a_raw.at[0])
    ld_r0 = load(r_hbm.at[0, 0], v.r_raw.at[0])
    rest = pl.ds(1, LEVELS - 1)
    ld_a = load(a_hbm.at[rest, 0], v.a_raw.at[rest])
    ld_r = load(r_hbm.at[rest, 0], v.r_raw.at[rest])
    ld_p = load(p_hbm.at[:, 0], v.p_raw)
    ld_i = load(inv_hbm, v.cinv)

    n_rem = [0]
    started = []

    def remote(src, dst, where, sends=None, recvs=None):
        idx = n_rem[0]
        n_rem[0] += 1
        copy = pltpu.make_async_remote_copy(
            src_ref=src, dst_ref=dst, send_sem=v.send_sem.at[idx], recv_sem=v.recv_sem.at[idx],
            device_id=where, device_id_type=pl.DeviceIdType.MESH,
        )
        if sends is None:
            copy.start()
        else:
            pl.when(sends)(copy.start)
        started.append((copy, sends))
        return copy, recvs

    def arrived(item):
        copy, recvs = item
        if recvs is None:
            copy.wait_recv()
        else:
            pl.when(recvs)(copy.wait_recv)

    lane = lax.broadcasted_iota(jnp.int32, (BS, 2 * BS), 1)
    row = lax.broadcasted_iota(jnp.int32, (BS, 2 * BS), 0)
    upper = lane // BS
    on_low = row == lane
    on_high = row + BS == lane
    halo_lo = jnp.where(upper == 0, jnp.where(has_prev, NB, -1), -1)
    halo_hi = jnp.where(upper == 1, jnp.where(has_next, NB + 1, -1), -1)

    def doubled(block):
        wide = block.astype(f32)
        return jnp.concatenate([wide, wide], axis=1)

    def pick(code, ids, blocks):
        total = jnp.where(code == ids[0], blocks[0], 0.0)
        for c, blk in zip(ids[1:], blocks[1:]):
            total = total + jnp.where(code == c, blk, 0.0)
        return total.astype(bf16)

    def each_block(body):
        def step(b, carry):
            body(b, pl.ds(pl.multiple_of(b * BS, BS), BS))
            return carry

        lax.fori_loop(0, NB, step, 0)

    def two_diagonals(k, low, high):
        picked = jnp.where(on_low, doubled(v.a_raw[k, low, 0]), 0.0)
        picked = picked + jnp.where(on_high, doubled(v.a_raw[k, high, 0]), 0.0)
        return 1.0 / jnp.sum(picked, axis=0, keepdims=True)

    def prep_diag(k):
        v.dsend[k] = jnp.broadcast_to(two_diagonals(k, 3, 0), (8, 128))
        v.drow[k, 0:1, 0:128] = two_diagonals(k, 0, 1)
        v.drow[k, 0:1, 128:256] = two_diagonals(k, 2, 3)

    def prep_t(k):
        def body(b, at):
            ids = [v.gcol[0, s, b, k] for s in range(5)]
            blocks = [doubled(v.a_raw[k, b, s]) for s in range(5)]
            v.a_cat[k, at, 0:128] = pick(upper, ids, blocks)
            v.a_cat[k, at, 128:256] = pick(upper + 2, ids, blocks)
            v.a_cat[k, at, 256:384] = pick(halo_lo, ids, blocks)
            v.a_cat[k, at, 384:512] = pick(halo_hi, ids, blocks)
            ids = [v.rcol[0, s, b, k] for s in range(3)]
            blocks = [doubled(v.r_raw[k, b, s]) for s in range(3)]
            v.r_own[at, 0:128] = pick(upper + NB * bits[k], ids, blocks)
            v.r_own[at, 128:256] = pick(upper + (2 + NB * bits[k]), ids, blocks)

        each_block(body)
        restrict = v.r_own[...]
        inner = dot_nn(restrict, v.a_cat[k, :, 0:256])
        own = (restrict.astype(f32) - relax_down * inner * v.drow[k, 0:1, :]).astype(bf16)
        v.tmat[k, 0:256, 0:256] = own
        v.tmat[k, 256:320, 0:256] = own[192:256]
        v.tmat[k, 320:384, 0:256] = own[0:64]
        outer = -relax_down * dot_nn(restrict, v.a_cat[k, :, 256:512])
        if k > 0:
            scale = jnp.concatenate([v.dhalo[0, k, 0:1, :], v.dhalo[1, k, 0:1, :]], axis=1)
            outer = outer * scale
        outer = outer.astype(bf16)
        v.tmat[k, 0:256, 256:512] = outer
        v.tmat[k, 256:320, 256:512] = outer[192:256]
        v.tmat[k, 320:384, 256:512] = outer[0:64]

    def prep_m(k):
        def body(b, at):
            ids = [v.pcol[0, b, s, k] for s in range(2)]
            blocks = [doubled(v.p_raw[k, b, s]) for s in range(2)]
            v.p_own[at, 0:128] = pick(upper, ids, blocks)
            v.p_own[at, 128:256] = pick(upper + 2, ids, blocks)
            d = jnp.sum(jnp.where(on_low, doubled(v.a_raw[k, b, 0]), 0.0), axis=1, keepdims=True)
            v.dcol[k, at, :] = jnp.broadcast_to(1.0 / d, (BS, 128))

        each_block(body)
        prolong = v.p_own[...]
        inner = dot_nn(v.a_cat[k, :, 0:256], prolong)
        scale = jnp.concatenate([v.dcol[k], v.dcol[k]], axis=1)
        v.mmat[k] = (prolong.astype(f32) - relax_up * scale * inner).astype(bf16)

    def smoothed_twice(k):
        b = v.__dict__[f"b32_{k}"][...]
        dinv = v.drow[k, 0:1, :]
        s = relax_down * b * dinv
        return s + relax_up * (b - dot_nt(s.astype(bf16), v.a_cat[k, :, 0:256])) * dinv

    def share(k):
        n, m = FIELDS[k], FIELDS[k + 1]
        if m == n:
            return pl.ds(0, n), pl.ds(0, n)
        keep = pl.ds(pl.multiple_of(bits[k] * m, m), m)
        give = pl.ds(pl.multiple_of((1 - bits[k]) * m, m), m)
        return keep, give

    def own_rows(k):
        start = 0
        for t in range(min(k, SPLITS)):
            start = start + bits[t] * FIELDS[t + 1]
        return pl.ds(pl.multiple_of(start, FIELDS[k]), FIELDS[k]) if k else pl.ds(0, ALL)

    def no_halo(side):
        v.h_recv[side] = jnp.zeros((ALL, 128), bf16)
        v.dhalo[side] = jnp.zeros((LEVELS, 8, 128), f32)
        for k in range(LEVELS - 1):
            ref = v.__dict__[f"erecv{k}"]
            zeros = jnp.zeros((FIELDS[k + 1], 128), bf16)
            ref[side] = zeros
            ref[2 + side] = zeros

    pl.when(j == 0)(lambda: no_halo(0))
    pl.when(j == PIECES - 1)(lambda: no_halo(1))

    ld_a0.wait()
    prep_diag(0)
    ld_b.wait()
    for c in range(4):
        cols = slice(c * 128, (c + 1) * 128)
        edge = jnp.concatenate([v.b_std[192:256, cols], v.b_std[0:64, cols]], axis=0)
        v.h_send[cols, :] = (jnp.transpose(edge) * v.dsend[0, 0:1, :]).astype(bf16)
    pl.semaphore_wait(barrier, len(greeted))
    halo = [
        remote(v.h_send, v.h_recv.at[0], {"narrow": nxt}, has_next, has_prev),
        remote(v.h_send, v.h_recv.at[1], {"narrow": prv}, has_prev, has_next),
    ]
    ld_a.wait()
    for k in range(1, LEVELS):
        prep_diag(k)
    diags = [
        remote(v.dsend, v.dhalo.at[0], {"narrow": nxt}, has_next, has_prev),
        remote(v.dsend, v.dhalo.at[1], {"narrow": prv}, has_prev, has_next),
    ]
    for c in range(4):
        cols = slice(c * 128, (c + 1) * 128)
        v.bcat0[cols, 0:256] = jnp.transpose(v.b_std[:, cols]).astype(bf16)
    ld_g.wait()
    ld_rc.wait()
    ld_r0.wait()
    prep_t(0)
    for item in halo:
        arrived(item)
    v.bcat0[:, 256:384] = v.h_recv[0]
    v.bcat0[:, 384:512] = v.h_recv[1]

    def idle_work(k):
        if k == 0:
            ld_r.wait()
            for item in diags:
                arrived(item)
        if k + 1 < LEVELS:
            prep_t(k + 1)
        if k == 0:
            ld_pc.wait()
            ld_p.wait()
        prep_m(k)
        if 1 <= k < SPLITS:
            c_bf = smoothed_twice(k).astype(bf16)
            v.__dict__[f"cfull{k}"][own_rows(k), :] = c_bf
        if k == SPLITS:
            v.ctot[...] = smoothed_twice(k)
            v.deep[...] = v.mmat[k]
        if k > SPLITS:
            v.ctot[...] += dot_nt(smoothed_twice(k).astype(bf16), v.deep[...])
            v.deep[...] = dot_nn(v.deep[...], v.mmat[k]).astype(bf16)
        if k == LEVELS - 1:
            ld_i.wait()
            v.kmat[...] = dot_nn(v.deep[...], v.cinv[...]).astype(bf16)

    shared = {}
    for k in range(LEVELS):
        n, m = FIELDS[k], FIELDS[k + 1]
        bcat, pown, psend, precv = (v.__dict__[f"{x}{k}"] for x in ("bcat", "pown", "psend", "precv"))
        keep, give = share(k)
        wide_out = ROWS + 128 if k < LEVELS - 1 else ROWS
        weights = v.tmat[k, 0:wide_out, :]
        there = {"wide": partners[k]}
        pieces = []
        p = dot_nt(bcat[give, :], weights)
        psend[...] = p[:, 0:ROWS].astype(bf16)
        if k < LEVELS - 1:
            egive, ekeep, erecv = (v.__dict__[f"{x}{k}"] for x in ("egive", "ekeep", "erecv"))
            egive[...] = p[:, ROWS:].astype(bf16)
            pieces.append(remote(egive, erecv.at[2], {"wide": partners[k], "narrow": nxt}, has_next, has_prev))
            pieces.append(remote(egive, erecv.at[3], {"wide": partners[k], "narrow": prv}, has_prev, has_next))
        pieces.append(remote(psend, precv, there))
        if m < n:
            p = dot_nt(bcat[keep, :], weights)
            if k < LEVELS - 1:
                ekeep[...] = p[:, ROWS:].astype(bf16)
                edge = ekeep
        elif k < LEVELS - 1:
            edge = egive
        if k < LEVELS - 1:
            pieces.append(remote(edge, erecv.at[0], {"narrow": nxt}, has_next, has_prev))
            pieces.append(remote(edge, erecv.at[1], {"narrow": prv}, has_prev, has_next))
        pown[...] = p[:, 0:ROWS]
        idle_work(k)
        if k == SPLITS:
            for t in range(1, SPLITS):
                rows = own_rows(t)
                ref = v.__dict__[f"cfull{t}"]
                shared[t] = [
                    remote(ref.at[rows], ref.at[rows], {"wide": across(mask)}) for mask in range(1, 1 << t)
                ]
        for item in pieces:
            arrived(item)
        total = pown[...] + precv[...].astype(f32)
        if k < LEVELS - 1:
            after = v.__dict__[f"bcat{k + 1}"]
            v.__dict__[f"b32_{k + 1}"][...] = total
            after[:, 0:256] = total.astype(bf16)
            after[:, 256:384] = (erecv[0].astype(f32) + erecv[2].astype(f32)).astype(bf16)
            after[:, 384:512] = (erecv[1].astype(f32) + erecv[3].astype(f32)).astype(bf16)
        else:
            v.b7[0] = total.astype(bf16)

    gathers = [
        remote(v.b7.at[0], v.b7.at[d], {"narrow": lax.rem(j + PIECES - d, PIECES)}) for d in (2, 1, 3)
    ]

    def inverse_cols(d):
        return v.kmat[:, pl.ds(pl.multiple_of(lax.rem(j + d, PIECES) * ROWS, ROWS), ROWS)]

    b = v.b_std[...]
    dinv = jnp.concatenate([v.dcol[0]] * 4, axis=1)
    s = relax_down * b * dinv
    v.c_std[...] = s + relax_up * (b - dot_nn(v.a_cat[0, :, 0:256], s.astype(bf16))) * dinv
    v.fine[...] = v.mmat[0]
    for t in range(1, SPLITS):
        for item in shared[t]:
            arrived(item)
        v.c_std[...] += dot_nt(v.fine[...], v.__dict__[f"cfull{t}"][...])
        v.fine[...] = dot_nn(v.fine[...], v.mmat[t]).astype(bf16)
    v.ctot[...] += dot_nt(v.b7[0], inverse_cols(0))
    for item in gathers:
        arrived(item)
    x = v.ctot[...]
    for d in (1, 2, 3):
        x = x + dot_nt(v.b7[d], inverse_cols(d))

    rows = own_rows(SPLITS)
    v.xg[rows, :] = x.astype(bf16)
    handed = [
        remote(v.xg.at[rows], v.xg.at[rows], {"wide": across(mask)}) for mask in reversed(mates)
    ]
    for item in handed:
        arrived(item)
    outs = []
    for c in range(4):
        cols = slice(c * 128, (c + 1) * 128)
        v.outv[:, cols] = v.c_std[:, cols] + dot_nt(v.fine[...], v.xg[cols, :])
        copy = pltpu.make_async_copy(v.outv.at[:, cols], out_hbm.at[0, :, cols], v.out_sem.at[c])
        copy.start()
        outs.append(copy)
    for copy, sends in started:
        if sends is None:
            copy.wait_send()
        else:
            pl.when(sends)(copy.wait_send)
    for copy in outs:
        copy.wait()


def on_device(rhs, gcol, galerkin, rcol, restrict, pcol, prolong, inverse):
    hbm = pl.BlockSpec(memory_space=pl.ANY)
    return pl.pallas_call(
        kernel,
        out_shape=jax.ShapeDtypeStruct(rhs.shape, f32),
        in_specs=[hbm] * 8,
        out_specs=hbm,
        scratch_shapes=list(scratch_specs().values()),
        compiler_params=pltpu.CompilerParams(
            collective_id=0, has_side_effects=True, vmem_limit_bytes=60 * 1024 * 1024
        ),
    )(
        jnp.transpose(gcol, (1, 3, 2, 0)),
        jnp.transpose(rcol, (1, 3, 2, 0)),
        jnp.transpose(pcol, (1, 2, 3, 0)),
        rhs, galerkin, restrict, prolong, inverse,
    )


def solution(mesh):
    in_specs = (
        P("wide", "narrow", None),
        P(None, "wide", "narrow", None),
        P(None, "wide", "narrow", None, None, None),
        P(None, "wide", "narrow", None),
        P(None, "wide", "narrow", None, None, None),
        P(None, "wide", "narrow", None),
        P(None, "wide", "narrow", None, None, None),
        P("narrow", None),
    )
    out_specs = P("wide", "narrow", None)
    return jax.shard_map(
        on_device, mesh=mesh, in_specs=in_specs, out_specs=out_specs, check_vma=False
    )
```

```python
import jax
import jax.numpy as jnp
from jax import lax
from jax.experimental import pallas as pl
from jax.experimental.pallas import tpu as pltpu
from jax.sharding import PartitionSpec as P

relax_down = 0.7
relax_up = 0.5

LEVELS = 7
SPLITS = 4
BS = 64
NB = 4
ROWS = NB * BS
ALL = 512
PIECES = 4
WIDE = ROWS + 2 * BS
REMOTES = 96

f32 = jnp.float32
bf16 = jnp.bfloat16
NT = (((1,), (1,)), ((), ()))
FIELDS = [ALL >> min(level, SPLITS) for level in range(LEVELS + 1)]


def dot_nn(a, b):
    return jnp.dot(a, b, preferred_element_type=f32)


def dot_nt(a, b):
    return lax.dot_general(a, b, NT, preferred_element_type=f32)


def scratch_specs():
    vmem, dma = pltpu.VMEM, pltpu.SemaphoreType.DMA
    specs = {
        "gcol": pltpu.SMEM((1, 5, NB, LEVELS), jnp.int32),
        "rcol": pltpu.SMEM((1, 3, NB, LEVELS), jnp.int32),
        "pcol": pltpu.SMEM((1, NB, 2, LEVELS), jnp.int32),
        "b_std": vmem((ROWS, ALL), f32),
        "a_raw": vmem((LEVELS, NB, 5, BS, BS), bf16),
        "r_raw": vmem((LEVELS, NB, 3, BS, BS), bf16),
        "p_raw": vmem((LEVELS, NB, 2, BS, BS), bf16),
        "cinv": vmem((ROWS, PIECES * ROWS), bf16),
        "a_cat": vmem((LEVELS, ROWS, WIDE), bf16),
        "r_own": vmem((ROWS, ROWS), bf16),
        "p_own": vmem((ROWS, ROWS), bf16),
        "tmat": vmem((LEVELS, WIDE, WIDE), bf16),
        "mmat": vmem((LEVELS, ROWS, ROWS), bf16),
        "deep": vmem((ROWS, ROWS), bf16),
        "fine": vmem((ROWS, ROWS), bf16),
        "kmat": vmem((PIECES * ROWS, ROWS), bf16),
        "drow": vmem((LEVELS, 8, ROWS), f32),
        "dcol": vmem((LEVELS, ROWS, 128), f32),
        "dsend": vmem((LEVELS, 8, 128), f32),
        "dhalo": vmem((2, LEVELS, 8, 128), f32),
        "edges": vmem((2 * BS, ALL), f32),
        "edge_diag": vmem((2, BS, BS), bf16),
        "h_send": vmem((2 * BS, ALL), bf16),
        "h_recv": vmem((2 * BS, ALL), bf16),
        "first": vmem((ALL, WIDE), f32),
        "ctot": vmem((FIELDS[LEVELS], ROWS), f32),
        "c_std": vmem((ROWS, ALL), f32),
        "b7": vmem((PIECES, FIELDS[LEVELS], ROWS), bf16),
        "xg": vmem((ALL, ROWS), bf16),
        "outv": vmem((ROWS, ALL), f32),
        "load_sem": dma((32,)),
        "out_sem": dma((4,)),
        "send_sem": dma((REMOTES,)),
        "recv_sem": dma((REMOTES,)),
        "far_sem": pltpu.SemaphoreType.REGULAR((3, 2)),
    }
    for k in range(LEVELS):
        n, m = FIELDS[k], FIELDS[k + 1]
        specs[f"bcat{k}"] = vmem((n, WIDE), bf16)
        specs[f"b32_{k + 1}"] = vmem((m, ROWS), f32)
        specs[f"pown{k}"] = vmem((m, ROWS), f32)
        specs[f"psend{k}"] = vmem((m, ROWS), bf16)
        specs[f"precv{k}"] = vmem((m, ROWS), bf16)
        if k < LEVELS - 1:
            specs[f"egive{k}"] = vmem((m, 128), bf16)
            specs[f"ekeep{k}"] = vmem((m, 128), bf16)
            specs[f"erecv{k}"] = vmem((4, m, 128), bf16)
        if 1 <= k < SPLITS:
            specs[f"cfull{k}"] = vmem((ALL, ROWS), bf16)
    return specs


class Refs:
    pass


def kernel(gcol_hbm, rcol_hbm, pcol_hbm, rhs_hbm, a_hbm, r_hbm, p_hbm, inv_hbm, out_hbm, *refs):
    v = Refs()
    for name, ref in zip(scratch_specs(), refs):
        setattr(v, name, ref)
    w = lax.axis_index("wide")
    j = lax.axis_index("narrow")
    nxt = lax.rem(j + 1, PIECES)
    prv = lax.rem(j + PIECES - 1, PIECES)
    has_next = j < PIECES - 1
    has_prev = j > 0
    bits = [lax.rem(w // (1 << k), 2) for k in range(LEVELS)]

    def across(mask):
        other = w
        for k in range(LEVELS):
            if mask >> k & 1:
                other = other + (1 - 2 * bits[k]) * (1 << k)
        return other

    partners = [across(1 << k) for k in range(LEVELS)]
    mates = range(1, 1 << SPLITS)

    def ring(distance):
        size = lax.axis_size("wide")
        return lax.rem(w + distance, size), lax.rem(w + size - distance, size)

    barrier = pltpu.get_barrier_semaphore()
    greeted = [{"narrow": lax.rem(j + d, PIECES)} for d in (1, 2, 3)]
    greeted += [{"wide": p} for p in partners[:3]]
    greeted += [{"wide": p} for p in ring(8)]
    for where in greeted:
        pl.semaphore_signal(barrier, inc=1, device_id=where)

    def pass_on(stage):
        up, down = ring(8 << stage)
        pl.semaphore_signal(v.far_sem.at[stage, 0], inc=1, device_id={"wide": up})
        pl.semaphore_signal(v.far_sem.at[stage, 1], inc=1, device_id={"wide": down})

    def passed(stage):
        pl.semaphore_wait(v.far_sem.at[stage, 0], 1)
        pl.semaphore_wait(v.far_sem.at[stage, 1], 1)

    n_load = [0]

    def load(src, dst):
        copy = pltpu.make_async_copy(src, dst, v.load_sem.at[n_load[0]])
        n_load[0] += 1
        copy.start()
        return copy

    ld_e = [
        load(a_hbm.at[0, 0, 3, 0], v.edge_diag.at[0]),
        load(a_hbm.at[0, 0, 0, 0], v.edge_diag.at[1]),
        load(rhs_hbm.at[0, 192:256], v.edges.at[0:64]),
        load(rhs_hbm.at[0, 0:64], v.edges.at[64:128]),
    ]
    ld_b = load(rhs_hbm.at[0], v.b_std)
    ld_g = load(gcol_hbm, v.gcol)
    ld_rc = load(rcol_hbm, v.rcol)
    ld_pc = load(pcol_hbm, v.pcol)
    ld_a0 = load(a_hbm.at[0, 0], v.a_raw.at[0])
    ld_r0 = load(r_hbm.at[0, 0], v.r_raw.at[0])
    rest = pl.ds(1, LEVELS - 1)
    ld_a = load(a_hbm.at[rest, 0], v.a_raw.at[rest])
    ld_r = load(r_hbm.at[rest, 0], v.r_raw.at[rest])
    ld_p = load(p_hbm.at[:, 0], v.p_raw)
    ld_i = load(inv_hbm, v.cinv)

    n_rem = [0]
    started = []

    def remote(src, dst, where, sends=None, recvs=None):
        idx = n_rem[0]
        n_rem[0] += 1
        copy = pltpu.make_async_remote_copy(
            src_ref=src, dst_ref=dst, send_sem=v.send_sem.at[idx], recv_sem=v.recv_sem.at[idx],
            device_id=where, device_id_type=pl.DeviceIdType.MESH,
        )
        if sends is None:
            copy.start()
        else:
            pl.when(sends)(copy.start)
        started.append((copy, sends))
        return copy, recvs

    def arrived(item):
        copy, recvs = item
        if recvs is None:
            copy.wait_recv()
        else:
            pl.when(recvs)(copy.wait_recv)

    lane = lax.broadcasted_iota(jnp.int32, (BS, 2 * BS), 1)
    row = lax.broadcasted_iota(jnp.int32, (BS, 2 * BS), 0)
    upper = lane // BS
    on_low = row == lane
    on_high = row + BS == lane
    halo_code = jnp.where(upper == 0, jnp.where(has_prev, NB, -1), jnp.where(has_next, NB + 1, -1))

    def doubled(block):
        wide = block.astype(f32)
        return jnp.concatenate([wide, wide], axis=1)

    def pick(code, ids, blocks):
        total = jnp.where(code == ids[0], blocks[0], 0.0)
        for c, blk in zip(ids[1:], blocks[1:]):
            total = total + jnp.where(code == c, blk, 0.0)
        return total.astype(bf16)

    def each_block(body):
        def step(b, carry):
            body(b, pl.ds(pl.multiple_of(b * BS, BS), BS))
            return carry

        lax.fori_loop(0, NB, step, 0)

    def two_diagonals(k, low, high):
        picked = jnp.where(on_low, doubled(v.a_raw[k, low, 0]), 0.0)
        picked = picked + jnp.where(on_high, doubled(v.a_raw[k, high, 0]), 0.0)
        return 1.0 / jnp.sum(picked, axis=0, keepdims=True)

    def prep_diag(k):
        v.dsend[k] = jnp.broadcast_to(two_diagonals(k, 3, 0), (8, 128))
        v.drow[k, 0:1, 0:128] = two_diagonals(k, 0, 1)
        v.drow[k, 0:1, 128:256] = two_diagonals(k, 2, 3)

    def prep_t(k):
        def body(b, at):
            ids = [v.gcol[0, s, b, k] for s in range(5)]
            blocks = [doubled(v.a_raw[k, b, s]) for s in range(5)]
            v.a_cat[k, at, 0:128] = pick(upper, ids, blocks)
            v.a_cat[k, at, 128:256] = pick(upper + 2, ids, blocks)
            v.a_cat[k, at, 256:384] = pick(halo_code, ids, blocks)
            ids = [v.rcol[0, s, b, k] for s in range(3)]
            blocks = [doubled(v.r_raw[k, b, s]) for s in range(3)]
            v.r_own[at, 0:128] = pick(upper + NB * bits[k], ids, blocks)
            v.r_own[at, 128:256] = pick(upper + (2 + NB * bits[k]), ids, blocks)

        each_block(body)
        restrict = v.r_own[...]
        inner = dot_nn(restrict, v.a_cat[k])
        own = restrict.astype(f32) - relax_down * inner[:, 0:256] * v.drow[k, 0:1, :]
        outer = -relax_down * inner[:, 256:384]
        if k > 0:
            outer = outer * jnp.where(upper[0:1] == 0, v.dhalo[0, k, 0:1, :], v.dhalo[1, k, 0:1, :])
        for at, part in ((slice(0, 128), own[:, 0:128]), (slice(128, 256), own[:, 128:256]), (slice(256, 384), outer)):
            v.tmat[k, at, 0:256] = jnp.transpose(part).astype(bf16)
            ends = jnp.concatenate([part[192:256], part[0:64]], axis=0)
            v.tmat[k, at, 256:384] = jnp.transpose(ends).astype(bf16)

    def prep_m(k):
        def body(b, at):
            ids = [v.pcol[0, b, s, k] for s in range(2)]
            blocks = [doubled(v.p_raw[k, b, s]) for s in range(2)]
            v.p_own[at, 0:128] = pick(upper, ids, blocks)
            v.p_own[at, 128:256] = pick(upper + 2, ids, blocks)
            d = jnp.sum(jnp.where(on_low, doubled(v.a_raw[k, b, 0]), 0.0), axis=1, keepdims=True)
            v.dcol[k, at, :] = jnp.broadcast_to(1.0 / d, (BS, 128))

        each_block(body)
        prolong = v.p_own[...]
        inner = dot_nn(v.a_cat[k, :, 0:256], prolong)
        scale = jnp.concatenate([v.dcol[k], v.dcol[k]], axis=1)
        v.mmat[k] = (prolong.astype(f32) - relax_up * scale * inner).astype(bf16)

    def smoothed_twice(k):
        b = v.__dict__[f"b32_{k}"][...]
        dinv = v.drow[k, 0:1, :]
        s = relax_down * b * dinv
        return s + relax_up * (b - dot_nt(s.astype(bf16), v.a_cat[k, :, 0:256])) * dinv

    def share(k):
        n, m = FIELDS[k], FIELDS[k + 1]
        if m == n:
            return pl.ds(0, n), pl.ds(0, n)
        keep = pl.ds(pl.multiple_of(bits[k] * m, m), m)
        give = pl.ds(pl.multiple_of((1 - bits[k]) * m, m), m)
        return keep, give

    def own_rows(k):
        start = 0
        for t in range(min(k, SPLITS)):
            start = start + bits[t] * FIELDS[t + 1]
        return pl.ds(pl.multiple_of(start, FIELDS[k]), FIELDS[k]) if k else pl.ds(0, ALL)

    def no_halo(side):
        v.h_recv[side * BS:(side + 1) * BS, :] = jnp.zeros((BS, ALL), bf16)
        v.dhalo[side] = jnp.zeros((LEVELS, 8, 128), f32)
        for k in range(LEVELS - 1):
            ref = v.__dict__[f"erecv{k}"]
            zeros = jnp.zeros((FIELDS[k + 1], 128), bf16)
            ref[side] = zeros
            ref[2 + side] = zeros

    pl.when(j == 0)(lambda: no_halo(0))
    pl.when(j == PIECES - 1)(lambda: no_halo(1))

    for copy in ld_e:
        copy.wait()
    for i in range(2):
        at = slice(i * BS, (i + 1) * BS)
        d = jnp.sum(jnp.where(on_low, doubled(v.edge_diag[i]), 0.0), axis=1, keepdims=True)
        v.h_send[at, :] = (v.edges[at, :] * (1.0 / d)).astype(bf16)
    pl.semaphore_wait(barrier, len(greeted))
    halo = [
        remote(v.h_send.at[0:64], v.h_recv.at[0:64], {"narrow": nxt}, has_next, has_prev),
        remote(v.h_send.at[64:128], v.h_recv.at[64:128], {"narrow": prv}, has_prev, has_next),
    ]
    pass_on(0)
    ld_a0.wait()
    ld_a.wait()
    for k in range(LEVELS):
        prep_diag(k)
    diags = [
        remote(v.dsend, v.dhalo.at[0], {"narrow": nxt}, has_next, has_prev),
        remote(v.dsend, v.dhalo.at[1], {"narrow": prv}, has_prev, has_next),
    ]
    ld_b.wait()
    for c in range(4):
        cols = slice(c * 128, (c + 1) * 128)
        v.bcat0[cols, 0:256] = jnp.transpose(v.b_std[:, cols]).astype(bf16)
    ld_g.wait()
    ld_rc.wait()
    ld_r0.wait()
    prep_t(0)
    v.first[...] = dot_nn(v.bcat0[:, 0:256], v.tmat[0, 0:256, :])
    for item in halo:
        arrived(item)
    for c in range(4):
        cols = slice(c * 128, (c + 1) * 128)
        v.bcat0[cols, 256:384] = jnp.transpose(v.h_recv[:, cols].astype(f32)).astype(bf16)

    def idle_work(k):
        if k < 3:
            passed(k)
            if k < 2:
                pass_on(k + 1)
        if k == 0:
            ld_r.wait()
            for item in diags:
                arrived(item)
        if k + 1 < LEVELS:
            prep_t(k + 1)
        if k == 0:
            ld_pc.wait()
            ld_p.wait()
        prep_m(k)
        if 1 <= k < SPLITS:
            c_bf = smoothed_twice(k).astype(bf16)
            v.__dict__[f"cfull{k}"][own_rows(k), :] = c_bf
        if k == SPLITS:
            v.ctot[...] = smoothed_twice(k)
            v.deep[...] = v.mmat[k]
        if k > SPLITS:
            v.ctot[...] += dot_nt(smoothed_twice(k).astype(bf16), v.deep[...])
            v.deep[...] = dot_nn(v.deep[...], v.mmat[k]).astype(bf16)
        if k == LEVELS - 1:
            ld_i.wait()
            for d in range(PIECES):
                at = slice(d * ROWS, (d + 1) * ROWS)
                v.kmat[at, :] = jnp.transpose(dot_nn(v.deep[...], v.cinv[:, at])).astype(bf16)

    shared = {}
    for k in range(LEVELS):
        n, m = FIELDS[k], FIELDS[k + 1]
        bcat, pown, psend, precv = (v.__dict__[f"{x}{k}"] for x in ("bcat", "pown", "psend", "precv"))
        keep, give = share(k)
        wide_out = ROWS + 128 if k < LEVELS - 1 else ROWS

        def product(rows):
            if k == 0:
                return v.first[rows, :] + dot_nn(bcat[rows, 256:384], v.tmat[0, 256:384, :])
            return dot_nn(bcat[rows, :], v.tmat[k, :, 0:wide_out])

        there = {"wide": partners[k]}
        pieces = []
        p = product(give)
        psend[...] = p[:, 0:ROWS].astype(bf16)
        if k < LEVELS - 1:
            egive, ekeep, erecv = (v.__dict__[f"{x}{k}"] for x in ("egive", "ekeep", "erecv"))
            egive[...] = p[:, ROWS:].astype(bf16)
            pieces.append(remote(egive, erecv.at[2], {"wide": partners[k], "narrow": nxt}, has_next, has_prev))
            pieces.append(remote(egive, erecv.at[3], {"wide": partners[k], "narrow": prv}, has_prev, has_next))
        pieces.append(remote(psend, precv, there))
        if m < n:
            p = product(keep)
            if k < LEVELS - 1:
                ekeep[...] = p[:, ROWS:].astype(bf16)
                edge = ekeep
        elif k < LEVELS - 1:
            edge = egive
        if k < LEVELS - 1:
            pieces.append(remote(edge, erecv.at[0], {"narrow": nxt}, has_next, has_prev))
            pieces.append(remote(edge, erecv.at[1], {"narrow": prv}, has_prev, has_next))
        pown[...] = p[:, 0:ROWS]
        idle_work(k)
        if k == SPLITS:
            for t in range(1, SPLITS):
                rows = own_rows(t)
                ref = v.__dict__[f"cfull{t}"]
                shared[t] = [
                    remote(ref.at[rows], ref.at[rows], {"wide": across(mask)}) for mask in range(1, 1 << t)
                ]
        for item in pieces:
            arrived(item)
        total = pown[...] + precv[...].astype(f32)
        if k < LEVELS - 1:
            after = v.__dict__[f"bcat{k + 1}"]
            v.__dict__[f"b32_{k + 1}"][...] = total
            after[:, 0:256] = total.astype(bf16)
            before = erecv[0].astype(f32) + erecv[2].astype(f32)
            behind = erecv[1].astype(f32) + erecv[3].astype(f32)
            side = lax.broadcasted_iota(jnp.int32, (m, 128), 1)
            after[:, 256:384] = jnp.where(side < BS, before, behind).astype(bf16)
        else:
            v.b7[0] = total.astype(bf16)

    gathers = [
        remote(v.b7.at[0], v.b7.at[d], {"narrow": lax.rem(j + PIECES - d, PIECES)}) for d in (2, 1, 3)
    ]

    def inverse_rows(d):
        return v.kmat[pl.ds(pl.multiple_of(lax.rem(j + d, PIECES) * ROWS, ROWS), ROWS), :]

    b = v.b_std[...]
    dinv = jnp.concatenate([v.dcol[0]] * 4, axis=1)
    s = relax_down * b * dinv
    v.c_std[...] = s + relax_up * (b - dot_nn(v.a_cat[0, :, 0:256], s.astype(bf16))) * dinv
    v.fine[...] = v.mmat[0]
    for t in range(1, SPLITS):
        for item in shared[t]:
            arrived(item)
        v.c_std[...] += dot_nt(v.fine[...], v.__dict__[f"cfull{t}"][...])
        v.fine[...] = dot_nn(v.fine[...], v.mmat[t]).astype(bf16)
    v.ctot[...] += dot_nn(v.b7[0], inverse_rows(0))
    for item in gathers:
        arrived(item)
    x = v.ctot[...]
    for d in (1, 2, 3):
        x = x + dot_nn(v.b7[d], inverse_rows(d))

    rows = own_rows(SPLITS)
    v.xg[rows, :] = x.astype(bf16)
    handed = [
        remote(v.xg.at[rows], v.xg.at[rows], {"wide": across(mask)}) for mask in reversed(mates)
    ]
    for item in handed:
        arrived(item)
    outs = []
    for c in range(4):
        cols = slice(c * 128, (c + 1) * 128)
        v.outv[:, cols] = v.c_std[:, cols] + dot_nt(v.fine[...], v.xg[cols, :])
        copy = pltpu.make_async_copy(v.outv.at[:, cols], out_hbm.at[0, :, cols], v.out_sem.at[c])
        copy.start()
        outs.append(copy)
    for copy, sends in started:
        if sends is None:
            copy.wait_send()
        else:
            pl.when(sends)(copy.wait_send)
    for copy in outs:
        copy.wait()


def on_device(rhs, gcol, galerkin, rcol, restrict, pcol, prolong, inverse):
    hbm = pl.BlockSpec(memory_space=pl.ANY)
    return pl.pallas_call(
        kernel,
        out_shape=jax.ShapeDtypeStruct(rhs.shape, f32),
        in_specs=[hbm] * 8,
        out_specs=hbm,
        scratch_shapes=list(scratch_specs().values()),
        compiler_params=pltpu.CompilerParams(
            collective_id=0, has_side_effects=True, vmem_limit_bytes=60 * 1024 * 1024
        ),
    )(
        jnp.transpose(gcol, (1, 3, 2, 0)),
        jnp.transpose(rcol, (1, 3, 2, 0)),
        jnp.transpose(pcol, (1, 2, 3, 0)),
        rhs, galerkin, restrict, prolong, inverse,
    )


def solution(mesh):
    in_specs = (
        P("wide", "narrow", None),
        P(None, "wide", "narrow", None),
        P(None, "wide", "narrow", None, None, None),
        P(None, "wide", "narrow", None),
        P(None, "wide", "narrow", None, None, None),
        P(None, "wide", "narrow", None),
        P(None, "wide", "narrow", None, None, None),
        P("narrow", None),
    )
    out_specs = P("wide", "narrow", None)
    return jax.shard_map(
        on_device, mesh=mesh, in_specs=in_specs, out_specs=out_specs, check_vma=False
    )
```

```python
import jax
import jax.numpy as jnp
from jax import lax
from jax.experimental import pallas as pl
from jax.experimental.pallas import tpu as pltpu
from jax.sharding import PartitionSpec as P

relax_down = 0.7
relax_up = 0.5

LEVELS = 7
SPLITS = 4
LAST = LEVELS - 1
JOINED = LEVELS - 2
BS = 64
NB = 4
ROWS = NB * BS
ALL = 512
PIECES = 4
WIDE = ROWS + 2 * BS
REMOTES = 96

f32 = jnp.float32
bf16 = jnp.bfloat16
NT = (((1,), (1,)), ((), ()))
FIELDS = [ALL >> min(level, SPLITS) for level in range(LEVELS + 1)]


def dot_nn(a, b):
    return jnp.dot(a, b, preferred_element_type=f32)


def dot_nt(a, b):
    return lax.dot_general(a, b, NT, preferred_element_type=f32)


def scratch_specs():
    vmem, dma = pltpu.VMEM, pltpu.SemaphoreType.DMA
    specs = {
        "gcol": pltpu.SMEM((1, 5, NB, LEVELS), jnp.int32),
        "rcol": pltpu.SMEM((1, 3, NB, LEVELS), jnp.int32),
        "pcol": pltpu.SMEM((1, NB, 2, LEVELS), jnp.int32),
        "b_std": vmem((ROWS, ALL), f32),
        "a_raw": vmem((LEVELS, NB, 5, BS, BS), bf16),
        "r_raw": vmem((LEVELS, NB, 3, BS, BS), bf16),
        "p_raw": vmem((LEVELS, NB, 2, BS, BS), bf16),
        "cinv": vmem((ROWS, PIECES * ROWS), bf16),
        "a_cat": vmem((LEVELS, ROWS, WIDE), bf16),
        "r_own": vmem((ROWS, ROWS), bf16),
        "p_own": vmem((ROWS, ROWS), bf16),
        "tmat": vmem((LEVELS, WIDE, WIDE), bf16),
        "mmat": vmem((LEVELS, ROWS, ROWS), bf16),
        "deep": vmem((ROWS, ROWS), bf16),
        "fine": vmem((ROWS, ROWS), bf16),
        "deep_t": vmem((ROWS, ROWS), bf16),
        "last_t": vmem((PIECES, WIDE, ROWS), bf16),
        "zpart": vmem((PIECES, WIDE, ROWS), f32),
        "zmat": vmem((PIECES, ROWS, ROWS), bf16),
        "drow": vmem((LEVELS, 8, ROWS), f32),
        "dcol": vmem((LEVELS, ROWS, 128), f32),
        "dsend": vmem((LEVELS, 8, 128), f32),
        "dhalo": vmem((2, LEVELS, 8, 128), f32),
        "edges": vmem((2 * BS, ALL), f32),
        "edge_diag": vmem((2, BS, BS), bf16),
        "h_send": vmem((2 * BS, ALL), bf16),
        "h_recv": vmem((2 * BS, ALL), bf16),
        "first": vmem((ALL, WIDE), f32),
        "ctot": vmem((FIELDS[LEVELS], ROWS), f32),
        "c_std": vmem((ROWS, ALL), f32),
        "q_all": vmem((PIECES, FIELDS[LEVELS], ROWS), bf16),
        "q_own": vmem((FIELDS[LEVELS], ROWS), f32),
        "q_far": vmem((FIELDS[LEVELS], ROWS), bf16),
        "x_own": vmem((FIELDS[LEVELS], ROWS), f32),
        "x_send": vmem((FIELDS[LEVELS], ROWS), bf16),
        "x_recv": vmem((3, FIELDS[LEVELS], ROWS), bf16),
        "xg": vmem((ALL, ROWS), bf16),
        "outv": vmem((ROWS, ALL), f32),
        "load_sem": dma((32,)),
        "out_sem": dma((4,)),
        "send_sem": dma((REMOTES,)),
        "recv_sem": dma((REMOTES,)),
        "far_sem": pltpu.SemaphoreType.REGULAR((3, 2)),
    }
    for k in range(LEVELS):
        n, m = FIELDS[k], FIELDS[k + 1]
        if k > 0:
            specs[f"b32_{k}"] = vmem((n, ROWS), f32)
        if k < LAST:
            specs[f"bcat{k}"] = vmem((n, WIDE), bf16)
        if k < JOINED:
            specs[f"pown{k}"] = vmem((m, ROWS), f32)
            specs[f"psend{k}"] = vmem((m, ROWS), bf16)
            specs[f"precv{k}"] = vmem((m, ROWS), bf16)
            specs[f"egive{k}"] = vmem((m, 128), bf16)
            specs[f"ekeep{k}"] = vmem((m, 128), bf16)
            specs[f"erecv{k}"] = vmem((4, m, 128), bf16)
        if 1 <= k < SPLITS:
            specs[f"cfull{k}"] = vmem((ALL, ROWS), bf16)
    return specs


class Refs:
    pass


def kernel(gcol_hbm, rcol_hbm, pcol_hbm, rhs_hbm, a_hbm, r_hbm, p_hbm, inv_hbm, out_hbm, *refs):
    v = Refs()
    for name, ref in zip(scratch_specs(), refs):
        setattr(v, name, ref)
    w = lax.axis_index("wide")
    j = lax.axis_index("narrow")
    nxt = lax.rem(j + 1, PIECES)
    prv = lax.rem(j + PIECES - 1, PIECES)
    has_next = j < PIECES - 1
    has_prev = j > 0
    bits = [lax.rem(w // (1 << k), 2) for k in range(LEVELS)]

    def across(mask):
        other = w
        for k in range(LEVELS):
            if mask >> k & 1:
                other = other + (1 - 2 * bits[k]) * (1 << k)
        return other

    partners = [across(1 << k) for k in range(LEVELS)]
    mates = range(1, 1 << SPLITS)

    def ring(distance):
        size = lax.axis_size("wide")
        return lax.rem(w + distance, size), lax.rem(w + size - distance, size)

    barrier = pltpu.get_barrier_semaphore()
    greeted = [{"narrow": lax.rem(j + d, PIECES)} for d in (1, 2, 3)]
    greeted += [{"wide": p} for p in partners[:3]]
    greeted += [{"wide": p} for p in ring(8)]
    for where in greeted:
        pl.semaphore_signal(barrier, inc=1, device_id=where)

    def pass_on(stage):
        up, down = ring(8 << stage)
        pl.semaphore_signal(v.far_sem.at[stage, 0], inc=1, device_id={"wide": up})
        pl.semaphore_signal(v.far_sem.at[stage, 1], inc=1, device_id={"wide": down})

    def passed(stage):
        pl.semaphore_wait(v.far_sem.at[stage, 0], 1)
        pl.semaphore_wait(v.far_sem.at[stage, 1], 1)

    n_load = [0]

    def load(src, dst):
        copy = pltpu.make_async_copy(src, dst, v.load_sem.at[n_load[0]])
        n_load[0] += 1
        copy.start()
        return copy

    ld_e = [
        load(a_hbm.at[0, 0, 3, 0], v.edge_diag.at[0]),
        load(a_hbm.at[0, 0, 0, 0], v.edge_diag.at[1]),
        load(rhs_hbm.at[0, 192:256], v.edges.at[0:64]),
        load(rhs_hbm.at[0, 0:64], v.edges.at[64:128]),
    ]
    ld_b = load(rhs_hbm.at[0], v.b_std)
    ld_g = load(gcol_hbm, v.gcol)
    ld_rc = load(rcol_hbm, v.rcol)
    ld_pc = load(pcol_hbm, v.pcol)
    ld_a0 = load(a_hbm.at[0, 0], v.a_raw.at[0])
    ld_r0 = load(r_hbm.at[0, 0], v.r_raw.at[0])
    rest = pl.ds(1, LEVELS - 1)
    ld_a = load(a_hbm.at[rest, 0], v.a_raw.at[rest])
    ld_r = load(r_hbm.at[rest, 0], v.r_raw.at[rest])
    ld_p = load(p_hbm.at[:, 0], v.p_raw)
    ld_i = load(inv_hbm, v.cinv)

    n_rem = [0]
    started = []

    def remote(src, dst, where, sends=None, recvs=None):
        idx = n_rem[0]
        n_rem[0] += 1
        copy = pltpu.make_async_remote_copy(
            src_ref=src, dst_ref=dst, send_sem=v.send_sem.at[idx], recv_sem=v.recv_sem.at[idx],
            device_id=where, device_id_type=pl.DeviceIdType.MESH,
        )
        if sends is None:
            copy.start()
        else:
            pl.when(sends)(copy.start)
        started.append((copy, sends))
        return copy, recvs

    def arrived(item):
        copy, recvs = item
        if recvs is None:
            copy.wait_recv()
        else:
            pl.when(recvs)(copy.wait_recv)

    lane = lax.broadcasted_iota(jnp.int32, (BS, 2 * BS), 1)
    row = lax.broadcasted_iota(jnp.int32, (BS, 2 * BS), 0)
    upper = lane // BS
    on_low = row == lane
    on_high = row + BS == lane
    halo_code = jnp.where(upper == 0, jnp.where(has_prev, NB, -1), jnp.where(has_next, NB + 1, -1))

    def doubled(block):
        wide = block.astype(f32)
        return jnp.concatenate([wide, wide], axis=1)

    def pick(code, ids, blocks):
        total = jnp.where(code == ids[0], blocks[0], 0.0)
        for c, blk in zip(ids[1:], blocks[1:]):
            total = total + jnp.where(code == c, blk, 0.0)
        return total.astype(bf16)

    def each_block(body):
        def step(b, carry):
            body(b, pl.ds(pl.multiple_of(b * BS, BS), BS))
            return carry

        lax.fori_loop(0, NB, step, 0)

    def two_diagonals(k, low, high):
        picked = jnp.where(on_low, doubled(v.a_raw[k, low, 0]), 0.0)
        picked = picked + jnp.where(on_high, doubled(v.a_raw[k, high, 0]), 0.0)
        return 1.0 / jnp.sum(picked, axis=0, keepdims=True)

    def prep_diag(k):
        v.dsend[k] = jnp.broadcast_to(two_diagonals(k, 3, 0), (8, 128))
        v.drow[k, 0:1, 0:128] = two_diagonals(k, 0, 1)
        v.drow[k, 0:1, 128:256] = two_diagonals(k, 2, 3)

    def prep_t(k):
        def body(b, at):
            ids = [v.gcol[0, s, b, k] for s in range(5)]
            blocks = [doubled(v.a_raw[k, b, s]) for s in range(5)]
            v.a_cat[k, at, 0:128] = pick(upper, ids, blocks)
            v.a_cat[k, at, 128:256] = pick(upper + 2, ids, blocks)
            v.a_cat[k, at, 256:384] = pick(halo_code, ids, blocks)
            ids = [v.rcol[0, s, b, k] for s in range(3)]
            blocks = [doubled(v.r_raw[k, b, s]) for s in range(3)]
            v.r_own[at, 0:128] = pick(upper + NB * bits[k], ids, blocks)
            v.r_own[at, 128:256] = pick(upper + (2 + NB * bits[k]), ids, blocks)

        each_block(body)
        restrict = v.r_own[...]
        inner = dot_nn(restrict, v.a_cat[k])
        own = restrict.astype(f32) - relax_down * inner[:, 0:256] * v.drow[k, 0:1, :]
        outer = -relax_down * inner[:, 256:384]
        if k > 0:
            outer = outer * jnp.where(upper[0:1] == 0, v.dhalo[0, k, 0:1, :], v.dhalo[1, k, 0:1, :])
        for at, part in ((slice(0, 128), own[:, 0:128]), (slice(128, 256), own[:, 128:256]), (slice(256, 384), outer)):
            v.tmat[k, at, 0:256] = jnp.transpose(part).astype(bf16)
            ends = jnp.concatenate([part[192:256], part[0:64]], axis=0)
            v.tmat[k, at, 256:384] = jnp.transpose(ends).astype(bf16)

    def prep_m(k):
        def body(b, at):
            ids = [v.pcol[0, b, s, k] for s in range(2)]
            blocks = [doubled(v.p_raw[k, b, s]) for s in range(2)]
            v.p_own[at, 0:128] = pick(upper, ids, blocks)
            v.p_own[at, 128:256] = pick(upper + 2, ids, blocks)
            d = jnp.sum(jnp.where(on_low, doubled(v.a_raw[k, b, 0]), 0.0), axis=1, keepdims=True)
            v.dcol[k, at, :] = jnp.broadcast_to(1.0 / d, (BS, 128))

        each_block(body)
        prolong = v.p_own[...]
        inner = dot_nn(v.a_cat[k, :, 0:256], prolong)
        scale = jnp.concatenate([v.dcol[k], v.dcol[k]], axis=1)
        v.mmat[k] = (prolong.astype(f32) - relax_up * scale * inner).astype(bf16)

    def smoothed_twice(k):
        b = v.__dict__[f"b32_{k}"][...]
        dinv = v.drow[k, 0:1, :]
        s = relax_down * b * dinv
        return s + relax_up * (b - dot_nt(s.astype(bf16), v.a_cat[k, :, 0:256])) * dinv

    def share(k):
        n, m = FIELDS[k], FIELDS[k + 1]
        if m == n:
            return pl.ds(0, n), pl.ds(0, n)
        keep = pl.ds(pl.multiple_of(bits[k] * m, m), m)
        give = pl.ds(pl.multiple_of((1 - bits[k]) * m, m), m)
        return keep, give

    def own_rows(k):
        start = 0
        for t in range(min(k, SPLITS)):
            start = start + bits[t] * FIELDS[t + 1]
        return pl.ds(pl.multiple_of(start, FIELDS[k]), FIELDS[k]) if k else pl.ds(0, ALL)

    def no_halo(side):
        v.h_recv[side * BS:(side + 1) * BS, :] = jnp.zeros((BS, ALL), bf16)
        v.dhalo[side] = jnp.zeros((LEVELS, 8, 128), f32)
        for k in range(JOINED):
            ref = v.__dict__[f"erecv{k}"]
            zeros = jnp.zeros((FIELDS[k + 1], 128), bf16)
            ref[side] = zeros
            ref[2 + side] = zeros

    pl.when(j == 0)(lambda: no_halo(0))
    pl.when(j == PIECES - 1)(lambda: no_halo(1))

    for copy in ld_e:
        copy.wait()
    for i in range(2):
        at = slice(i * BS, (i + 1) * BS)
        d = jnp.sum(jnp.where(on_low, doubled(v.edge_diag[i]), 0.0), axis=1, keepdims=True)
        v.h_send[at, :] = (v.edges[at, :] * (1.0 / d)).astype(bf16)
    pl.semaphore_wait(barrier, len(greeted))
    halo = [
        remote(v.h_send.at[0:64], v.h_recv.at[0:64], {"narrow": nxt}, has_next, has_prev),
        remote(v.h_send.at[64:128], v.h_recv.at[64:128], {"narrow": prv}, has_prev, has_next),
    ]
    pass_on(0)
    ld_a0.wait()
    ld_a.wait()
    for k in range(LEVELS):
        prep_diag(k)
    diags = [
        remote(v.dsend, v.dhalo.at[0], {"narrow": nxt}, has_next, has_prev),
        remote(v.dsend, v.dhalo.at[1], {"narrow": prv}, has_prev, has_next),
    ]
    ld_b.wait()
    for c in range(4):
        cols = slice(c * 128, (c + 1) * 128)
        v.bcat0[cols, 0:256] = jnp.transpose(v.b_std[:, cols]).astype(bf16)
    ld_g.wait()
    ld_rc.wait()
    ld_r0.wait()
    prep_t(0)
    v.first[...] = dot_nn(v.bcat0[:, 0:256], v.tmat[0, 0:256, :])
    for item in halo:
        arrived(item)
    for c in range(4):
        cols = slice(c * 128, (c + 1) * 128)
        v.bcat0[cols, 256:384] = jnp.transpose(v.h_recv[:, cols].astype(f32)).astype(bf16)

    def idle_work(k):
        if k < 3:
            passed(k)
            if k < 2:
                pass_on(k + 1)
        if k == 0:
            ld_r.wait()
            for item in diags:
                arrived(item)
        if k + 1 < LAST:
            prep_t(k + 1)
        if k == 0:
            prep_t(LAST)
            v.last_t[0] = v.tmat[LAST, :, 0:256]
        if k == 0:
            ld_pc.wait()
            ld_p.wait()
        prep_m(k)
        if 1 <= k < SPLITS:
            c_bf = smoothed_twice(k).astype(bf16)
            v.__dict__[f"cfull{k}"][own_rows(k), :] = c_bf
        if k == SPLITS:
            v.ctot[...] = smoothed_twice(k)
            v.deep[...] = v.mmat[k]
        if k > SPLITS:
            v.ctot[...] += dot_nt(smoothed_twice(k).astype(bf16), v.deep[...])
            v.deep[...] = dot_nn(v.deep[...], v.mmat[k]).astype(bf16)
        if k == JOINED - 1:
            ld_i.wait()
            for item in last_t:
                arrived(item)
            join_last()
        if k == LAST:
            v.deep_t[...] = jnp.transpose(v.deep[...].astype(f32)).astype(bf16)

    def join_last():
        for d in range(PIECES):
            cols = pl.ds(pl.multiple_of(lax.rem(j + d, PIECES) * ROWS, ROWS), ROWS)
            v.zpart[d] = dot_nt(v.last_t[d], v.cinv[:, cols])
        for d in range(PIECES):
            before, after = (d + PIECES - 1) % PIECES, (d + 1) % PIECES
            v.zmat[d, 0:64, :] = (v.zpart[d, 0:64, :] + v.zpart[before, 320:384, :]).astype(bf16)
            v.zmat[d, 64:192, :] = v.zpart[d, 64:192, :].astype(bf16)
            v.zmat[d, 192:256, :] = (v.zpart[d, 192:256, :] + v.zpart[after, 256:320, :]).astype(bf16)

    def to_pieces(ref, d):
        return remote(ref.at[0], ref.at[d], {"narrow": lax.rem(j + PIECES - d, PIECES)})

    last_t = []
    shared = {}
    for k in range(JOINED):
        n, m = FIELDS[k], FIELDS[k + 1]
        bcat, pown, psend, precv, egive, ekeep, erecv = (
            v.__dict__[f"{x}{k}"] for x in ("bcat", "pown", "psend", "precv", "egive", "ekeep", "erecv")
        )
        keep, give = share(k)

        def product(rows):
            if k == 0:
                return v.first[rows, :] + dot_nn(bcat[rows, 256:384], v.tmat[0, 256:384, :])
            return dot_nn(bcat[rows, :], v.tmat[k])

        p = product(give)
        psend[...] = p[:, 0:ROWS].astype(bf16)
        egive[...] = p[:, ROWS:].astype(bf16)
        pieces = [
            remote(egive, erecv.at[2], {"wide": partners[k], "narrow": nxt}, has_next, has_prev),
            remote(egive, erecv.at[3], {"wide": partners[k], "narrow": prv}, has_prev, has_next),
            remote(psend, precv, {"wide": partners[k]}),
        ]
        edge = egive
        if m < n:
            p = product(keep)
            ekeep[...] = p[:, ROWS:].astype(bf16)
            edge = ekeep
        pieces.append(remote(edge, erecv.at[0], {"narrow": nxt}, has_next, has_prev))
        pieces.append(remote(edge, erecv.at[1], {"narrow": prv}, has_prev, has_next))
        pown[...] = p[:, 0:ROWS]
        if k == 1:
            last_t += [to_pieces(v.last_t, d) for d in (1, 3)]
        if k == 2:
            last_t.append(to_pieces(v.last_t, 2))
        idle_work(k)
        if k == SPLITS:
            for t in range(1, SPLITS):
                rows = own_rows(t)
                ref = v.__dict__[f"cfull{t}"]
                shared[t] = [
                    remote(ref.at[rows], ref.at[rows], {"wide": across(mask)}) for mask in range(1, 1 << t)
                ]
        for item in pieces:
            arrived(item)
        total = pown[...] + precv[...].astype(f32)
        after = v.__dict__[f"bcat{k + 1}"]
        v.__dict__[f"b32_{k + 1}"][...] = total
        after[:, 0:256] = total.astype(bf16)
        before = erecv[0].astype(f32) + erecv[2].astype(f32)
        behind = erecv[1].astype(f32) + erecv[3].astype(f32)
        side = lax.broadcasted_iota(jnp.int32, (m, 128), 1)
        after[:, 256:384] = jnp.where(side < BS, before, behind).astype(bf16)

    k = JOINED
    v.q_own[...] = dot_nn(v.bcat5[...], v.tmat[k, :, 0:256])
    v.q_all[0] = v.q_own[...].astype(bf16)
    gathers = [to_pieces(v.q_all, d) for d in (2, 1, 3)]
    far = remote(v.q_all.at[0], v.q_far, {"wide": partners[k]})
    idle_work(k)
    v.x_own[...] = dot_nn(v.q_all[0], v.zmat[0])
    for item in gathers:
        arrived(item)
    x = v.x_own[...]
    for d in (1, 2, 3):
        x = x + dot_nn(v.q_all[d], v.zmat[d])
    v.x_send[...] = x.astype(bf16)
    sums = [
        remote(v.x_send, v.x_recv.at[i], {"wide": across(mask << k)}) for i, mask in enumerate((2, 3, 1))
    ]
    v.x_own[...] = x
    arrived(far)
    v.b32_6[...] = v.q_own[...] + v.q_far[...].astype(f32)
    idle_work(LAST)

    b = v.b_std[...]
    dinv = jnp.concatenate([v.dcol[0]] * 4, axis=1)
    s = relax_down * b * dinv
    v.c_std[...] = s + relax_up * (b - dot_nn(v.a_cat[0, :, 0:256], s.astype(bf16))) * dinv
    v.fine[...] = v.mmat[0]
    for t in range(1, SPLITS):
        for item in shared[t]:
            arrived(item)
        v.c_std[...] += dot_nt(v.fine[...], v.__dict__[f"cfull{t}"][...])
        v.fine[...] = dot_nn(v.fine[...], v.mmat[t]).astype(bf16)
    for item in sums:
        arrived(item)
    x = v.x_own[...] + v.x_recv[0].astype(f32) + v.x_recv[1].astype(f32) + v.x_recv[2].astype(f32)
    x = v.ctot[...] + dot_nn(x.astype(bf16), v.deep_t[...])

    rows = own_rows(SPLITS)
    v.xg[rows, :] = x.astype(bf16)
    handed = [
        remote(v.xg.at[rows], v.xg.at[rows], {"wide": across(mask)}) for mask in reversed(mates)
    ]
    for item in handed:
        arrived(item)
    outs = []
    for c in range(4):
        cols = slice(c * 128, (c + 1) * 128)
        v.outv[:, cols] = v.c_std[:, cols] + dot_nt(v.fine[...], v.xg[cols, :])
        copy = pltpu.make_async_copy(v.outv.at[:, cols], out_hbm.at[0, :, cols], v.out_sem.at[c])
        copy.start()
        outs.append(copy)
    for copy, sends in started:
        if sends is None:
            copy.wait_send()
        else:
            pl.when(sends)(copy.wait_send)
    for copy in outs:
        copy.wait()


def on_device(rhs, gcol, galerkin, rcol, restrict, pcol, prolong, inverse):
    hbm = pl.BlockSpec(memory_space=pl.ANY)
    return pl.pallas_call(
        kernel,
        out_shape=jax.ShapeDtypeStruct(rhs.shape, f32),
        in_specs=[hbm] * 8,
        out_specs=hbm,
        scratch_shapes=list(scratch_specs().values()),
        compiler_params=pltpu.CompilerParams(
            collective_id=0, has_side_effects=True, vmem_limit_bytes=60 * 1024 * 1024
        ),
    )(
        jnp.transpose(gcol, (1, 3, 2, 0)),
        jnp.transpose(rcol, (1, 3, 2, 0)),
        jnp.transpose(pcol, (1, 2, 3, 0)),
        rhs, galerkin, restrict, prolong, inverse,
    )


def solution(mesh):
    in_specs = (
        P("wide", "narrow", None),
        P(None, "wide", "narrow", None),
        P(None, "wide", "narrow", None, None, None),
        P(None, "wide", "narrow", None),
        P(None, "wide", "narrow", None, None, None),
        P(None, "wide", "narrow", None),
        P(None, "wide", "narrow", None, None, None),
        P("narrow", None),
    )
    out_specs = P("wide", "narrow", None)
    return jax.shard_map(
        on_device, mesh=mesh, in_specs=in_specs, out_specs=out_specs, check_vma=False
    )
```

```python
import jax
import jax.numpy as jnp
from jax import lax
from jax.experimental import pallas as pl
from jax.experimental.pallas import tpu as pltpu
from jax.sharding import PartitionSpec as P

relax_down = 0.7
relax_up = 0.5

LEVELS = 7
SPLITS = 4
LAST = LEVELS - 1
JOINED = LEVELS - 2
BS = 64
NB = 4
ROWS = NB * BS
ALL = 512
PIECES = 4
WIDE = ROWS + 2 * BS
REMOTES = 96

f32 = jnp.float32
bf16 = jnp.bfloat16
NT = (((1,), (1,)), ((), ()))
FIELDS = [ALL >> min(level, SPLITS) for level in range(LEVELS + 1)]


def dot_nn(a, b):
    return jnp.dot(a, b, preferred_element_type=f32)


def dot_nt(a, b):
    return lax.dot_general(a, b, NT, preferred_element_type=f32)


def scratch_specs():
    vmem, dma = pltpu.VMEM, pltpu.SemaphoreType.DMA
    specs = {
        "gcol": pltpu.SMEM((1, 5, NB, LEVELS), jnp.int32),
        "rcol": pltpu.SMEM((1, 3, NB, LEVELS), jnp.int32),
        "pcol": pltpu.SMEM((1, NB, 2, LEVELS), jnp.int32),
        "b_std": vmem((ROWS, ALL), f32),
        "a_raw": vmem((LEVELS, NB, 5, BS, BS), bf16),
        "r_raw": vmem((LEVELS, NB, 3, BS, BS), bf16),
        "p_raw": vmem((LEVELS, NB, 2, BS, BS), bf16),
        "cinv": vmem((ROWS, PIECES * ROWS), bf16),
        "a_cat": vmem((LEVELS, ROWS, WIDE), bf16),
        "r_own": vmem((ROWS, ROWS), bf16),
        "p_own": vmem((ROWS, ROWS), bf16),
        "tmat": vmem((LEVELS, WIDE, WIDE), bf16),
        "mmat": vmem((LEVELS, ROWS, ROWS), bf16),
        "deep": vmem((ROWS, ROWS), bf16),
        "fine": vmem((ROWS, ROWS), bf16),
        "deep_t": vmem((ROWS, ROWS), bf16),
        "last_t": vmem((PIECES, WIDE, ROWS), bf16),
        "zpart": vmem((PIECES, WIDE, ROWS), f32),
        "zmat": vmem((PIECES, ROWS, ROWS), bf16),
        "drow": vmem((LEVELS, 8, ROWS), f32),
        "dcol": vmem((LEVELS, ROWS, 128), f32),
        "dsend": vmem((LEVELS, 8, 128), f32),
        "dhalo": vmem((2, LEVELS, 8, 128), f32),
        "edges": vmem((2 * BS, ALL), f32),
        "edge_diag": vmem((2, BS, BS), bf16),
        "h_send": vmem((2 * BS, ALL), bf16),
        "h_recv": vmem((2 * BS, ALL), bf16),
        "first": vmem((ALL, WIDE), f32),
        "ctot": vmem((FIELDS[LEVELS], ROWS), f32),
        "c_std": vmem((ROWS, ALL), f32),
        "q_all": vmem((PIECES, FIELDS[LEVELS], ROWS), bf16),
        "q_own": vmem((FIELDS[LEVELS], ROWS), f32),
        "q_far": vmem((FIELDS[LEVELS], ROWS), bf16),
        "x_own": vmem((FIELDS[LEVELS], ROWS), f32),
        "x_send": vmem((FIELDS[LEVELS], ROWS), bf16),
        "x_recv": vmem((3, FIELDS[LEVELS], ROWS), bf16),
        "xg": vmem((ALL, ROWS), bf16),
        "load_sem": dma((32,)),
        "send_sem": dma((REMOTES,)),
        "recv_sem": dma((REMOTES,)),
        "far_sem": pltpu.SemaphoreType.REGULAR((3, 2)),
    }
    for k in range(LEVELS):
        n, m = FIELDS[k], FIELDS[k + 1]
        if k > 0:
            specs[f"b32_{k}"] = vmem((n, ROWS), f32)
        if k < LAST:
            specs[f"bcat{k}"] = vmem((n, WIDE), bf16)
        if k < JOINED:
            specs[f"pown{k}"] = vmem((m, ROWS), f32)
            specs[f"psend{k}"] = vmem((m, ROWS), bf16)
            specs[f"precv{k}"] = vmem((m, ROWS), bf16)
            specs[f"egive{k}"] = vmem((2, m // 2, 128), bf16)
            specs[f"ekeep{k}"] = vmem((2, m // 2, 128), bf16)
            specs[f"erecv{k}"] = vmem((4, m // 2, 128), bf16)
        if 1 <= k < SPLITS:
            specs[f"cfull{k}"] = vmem((ALL, ROWS), bf16)
    return specs


class Refs:
    pass


def kernel(gcol_hbm, rcol_hbm, pcol_hbm, rhs_hbm, a_hbm, r_hbm, p_hbm, inv_hbm, out, *refs):
    v = Refs()
    for name, ref in zip(scratch_specs(), refs):
        setattr(v, name, ref)
    w = lax.axis_index("wide")
    j = lax.axis_index("narrow")
    nxt = lax.rem(j + 1, PIECES)
    prv = lax.rem(j + PIECES - 1, PIECES)
    has_next = j < PIECES - 1
    has_prev = j > 0
    bits = [lax.rem(w // (1 << k), 2) for k in range(LEVELS)]

    def across(mask):
        other = w
        for k in range(LEVELS):
            if mask >> k & 1:
                other = other + (1 - 2 * bits[k]) * (1 << k)
        return other

    partners = [across(1 << k) for k in range(LEVELS)]
    mates = range(1, 1 << SPLITS)

    def ring(distance):
        size = lax.axis_size("wide")
        return lax.rem(w + distance, size), lax.rem(w + size - distance, size)

    barrier = pltpu.get_barrier_semaphore()
    greeted = [{"narrow": lax.rem(j + d, PIECES)} for d in (1, 2, 3)]
    greeted += [{"wide": p} for p in partners[:3]]
    greeted += [{"wide": p} for p in ring(8)]
    for where in greeted:
        pl.semaphore_signal(barrier, inc=1, device_id=where)

    def pass_on(stage):
        up, down = ring(8 << stage)
        pl.semaphore_signal(v.far_sem.at[stage, 0], inc=1, device_id={"wide": up})
        pl.semaphore_signal(v.far_sem.at[stage, 1], inc=1, device_id={"wide": down})

    def passed(stage):
        pl.semaphore_wait(v.far_sem.at[stage, 0], 1)
        pl.semaphore_wait(v.far_sem.at[stage, 1], 1)

    n_load = [0]

    def load(src, dst):
        copy = pltpu.make_async_copy(src, dst, v.load_sem.at[n_load[0]])
        n_load[0] += 1
        copy.start()
        return copy

    ld_e = [
        load(a_hbm.at[0, 0, 3, 0], v.edge_diag.at[0]),
        load(a_hbm.at[0, 0, 0, 0], v.edge_diag.at[1]),
        load(rhs_hbm.at[0, 192:256], v.edges.at[0:64]),
        load(rhs_hbm.at[0, 0:64], v.edges.at[64:128]),
    ]
    ld_b = load(rhs_hbm.at[0], v.b_std)
    ld_g = load(gcol_hbm, v.gcol)
    ld_rc = load(rcol_hbm, v.rcol)
    ld_pc = load(pcol_hbm, v.pcol)
    ld_a0 = load(a_hbm.at[0, 0], v.a_raw.at[0])
    ld_r0 = load(r_hbm.at[0, 0], v.r_raw.at[0])
    rest = pl.ds(1, LEVELS - 1)
    ld_a = load(a_hbm.at[rest, 0], v.a_raw.at[rest])
    ld_r = load(r_hbm.at[rest, 0], v.r_raw.at[rest])
    ld_p = load(p_hbm.at[:, 0], v.p_raw)
    ld_i = load(inv_hbm, v.cinv)

    n_rem = [0]
    started = []

    def remote(src, dst, where, sends=None, recvs=None):
        idx = n_rem[0]
        n_rem[0] += 1
        copy = pltpu.make_async_remote_copy(
            src_ref=src, dst_ref=dst, send_sem=v.send_sem.at[idx], recv_sem=v.recv_sem.at[idx],
            device_id=where, device_id_type=pl.DeviceIdType.MESH,
        )
        if sends is None:
            copy.start()
        else:
            pl.when(sends)(copy.start)
        started.append((copy, sends))
        return copy, recvs

    def arrived(item):
        copy, recvs = item
        if recvs is None:
            copy.wait_recv()
        else:
            pl.when(recvs)(copy.wait_recv)

    lane = lax.broadcasted_iota(jnp.int32, (BS, 2 * BS), 1)
    row = lax.broadcasted_iota(jnp.int32, (BS, 2 * BS), 0)
    upper = lane // BS
    on_low = row == lane
    on_high = row + BS == lane
    halo_code = jnp.where(upper == 0, jnp.where(has_prev, NB, -1), jnp.where(has_next, NB + 1, -1))

    def doubled(block):
        wide = block.astype(f32)
        return jnp.concatenate([wide, wide], axis=1)

    def pick(code, ids, blocks):
        total = jnp.where(code == ids[0], blocks[0], 0.0)
        for c, blk in zip(ids[1:], blocks[1:]):
            total = total + jnp.where(code == c, blk, 0.0)
        return total.astype(bf16)

    def each_block(body):
        def step(b, carry):
            body(b, pl.ds(pl.multiple_of(b * BS, BS), BS))
            return carry

        lax.fori_loop(0, NB, step, 0)

    def two_diagonals(k, low, high):
        picked = jnp.where(on_low, doubled(v.a_raw[k, low, 0]), 0.0)
        picked = picked + jnp.where(on_high, doubled(v.a_raw[k, high, 0]), 0.0)
        return 1.0 / jnp.sum(picked, axis=0, keepdims=True)

    def prep_diag(k):
        v.dsend[k] = jnp.broadcast_to(two_diagonals(k, 3, 0), (8, 128))
        v.drow[k, 0:1, 0:128] = two_diagonals(k, 0, 1)
        v.drow[k, 0:1, 128:256] = two_diagonals(k, 2, 3)

    def prep_t(k):
        def body(b, at):
            ids = [v.gcol[0, s, b, k] for s in range(5)]
            blocks = [doubled(v.a_raw[k, b, s]) for s in range(5)]
            v.a_cat[k, at, 0:128] = pick(upper, ids, blocks)
            v.a_cat[k, at, 128:256] = pick(upper + 2, ids, blocks)
            v.a_cat[k, at, 256:384] = pick(halo_code, ids, blocks)
            ids = [v.rcol[0, s, b, k] for s in range(3)]
            blocks = [doubled(v.r_raw[k, b, s]) for s in range(3)]
            v.r_own[at, 0:128] = pick(upper + NB * bits[k], ids, blocks)
            v.r_own[at, 128:256] = pick(upper + (2 + NB * bits[k]), ids, blocks)

        each_block(body)
        restrict = v.r_own[...]
        inner = dot_nn(restrict, v.a_cat[k])
        own = restrict.astype(f32) - relax_down * inner[:, 0:256] * v.drow[k, 0:1, :]
        outer = -relax_down * inner[:, 256:384]
        if k > 0:
            outer = outer * jnp.where(upper[0:1] == 0, v.dhalo[0, k, 0:1, :], v.dhalo[1, k, 0:1, :])
        for at, part in ((slice(0, 128), own[:, 0:128]), (slice(128, 256), own[:, 128:256]), (slice(256, 384), outer)):
            v.tmat[k, at, 0:256] = jnp.transpose(part).astype(bf16)
            ends = jnp.concatenate([part[192:256], part[0:64]], axis=0)
            v.tmat[k, at, 256:384] = jnp.transpose(ends).astype(bf16)

    def prep_m(k):
        def body(b, at):
            ids = [v.pcol[0, b, s, k] for s in range(2)]
            blocks = [doubled(v.p_raw[k, b, s]) for s in range(2)]
            v.p_own[at, 0:128] = pick(upper, ids, blocks)
            v.p_own[at, 128:256] = pick(upper + 2, ids, blocks)
            d = jnp.sum(jnp.where(on_low, doubled(v.a_raw[k, b, 0]), 0.0), axis=1, keepdims=True)
            v.dcol[k, at, :] = jnp.broadcast_to(1.0 / d, (BS, 128))

        each_block(body)
        prolong = v.p_own[...]
        inner = dot_nn(v.a_cat[k, :, 0:256], prolong)
        scale = jnp.concatenate([v.dcol[k], v.dcol[k]], axis=1)
        v.mmat[k] = (prolong.astype(f32) - relax_up * scale * inner).astype(bf16)

    def smoothed_twice(k):
        b = v.__dict__[f"b32_{k}"][...]
        dinv = v.drow[k, 0:1, :]
        s = relax_down * b * dinv
        return s + relax_up * (b - dot_nt(s.astype(bf16), v.a_cat[k, :, 0:256])) * dinv

    def share(k):
        n, m = FIELDS[k], FIELDS[k + 1]
        if m == n:
            return pl.ds(0, n), pl.ds(0, n)
        keep = pl.ds(pl.multiple_of(bits[k] * m, m), m)
        give = pl.ds(pl.multiple_of((1 - bits[k]) * m, m), m)
        return keep, give

    def own_rows(k):
        start = 0
        for t in range(min(k, SPLITS)):
            start = start + bits[t] * FIELDS[t + 1]
        return pl.ds(pl.multiple_of(start, FIELDS[k]), FIELDS[k]) if k else pl.ds(0, ALL)

    def no_halo(side):
        v.h_recv[side * BS:(side + 1) * BS, :] = jnp.zeros((BS, ALL), bf16)
        v.dhalo[side] = jnp.zeros((LEVELS, 8, 128), f32)
        for k in range(JOINED):
            ref = v.__dict__[f"erecv{k}"]
            zeros = jnp.zeros((FIELDS[k + 1] // 2, 128), bf16)
            ref[side] = zeros
            ref[2 + side] = zeros

    pl.when(j == 0)(lambda: no_halo(0))
    pl.when(j == PIECES - 1)(lambda: no_halo(1))

    for copy in ld_e:
        copy.wait()
    for i in range(2):
        at = slice(i * BS, (i + 1) * BS)
        d = jnp.sum(jnp.where(on_low, doubled(v.edge_diag[i]), 0.0), axis=1, keepdims=True)
        v.h_send[at, :] = (v.edges[at, :] * (1.0 / d)).astype(bf16)
    pl.semaphore_wait(barrier, len(greeted))
    halo = [
        remote(v.h_send.at[0:64], v.h_recv.at[0:64], {"narrow": nxt}, has_next, has_prev),
        remote(v.h_send.at[64:128], v.h_recv.at[64:128], {"narrow": prv}, has_prev, has_next),
    ]
    pass_on(0)
    ld_a0.wait()
    ld_a.wait()
    for k in range(LEVELS):
        prep_diag(k)
    diags = [
        remote(v.dsend, v.dhalo.at[0], {"narrow": nxt}, has_next, has_prev),
        remote(v.dsend, v.dhalo.at[1], {"narrow": prv}, has_prev, has_next),
    ]
    ld_b.wait()
    for c in range(4):
        cols = slice(c * 128, (c + 1) * 128)
        v.bcat0[cols, 0:256] = jnp.transpose(v.b_std[:, cols]).astype(bf16)
    ld_g.wait()
    ld_rc.wait()
    ld_r0.wait()
    prep_t(0)
    v.first[...] = dot_nn(v.bcat0[:, 0:256], v.tmat[0, 0:256, :])
    for item in halo:
        arrived(item)
    for c in range(4):
        cols = slice(c * 128, (c + 1) * 128)
        v.bcat0[cols, 256:384] = jnp.transpose(v.h_recv[:, cols].astype(f32)).astype(bf16)

    def idle_work(k):
        if k < 3:
            passed(k)
            if k < 2:
                pass_on(k + 1)
        if k == 0:
            ld_r.wait()
            for item in diags:
                arrived(item)
        if k + 1 < LAST:
            prep_t(k + 1)
        if k == 0:
            prep_t(LAST)
            v.last_t[0] = v.tmat[LAST, :, 0:256]
        if k == 0:
            ld_pc.wait()
            ld_p.wait()
        prep_m(k)
        if 1 <= k < SPLITS:
            c_bf = smoothed_twice(k).astype(bf16)
            v.__dict__[f"cfull{k}"][own_rows(k), :] = c_bf
        if k == SPLITS:
            v.ctot[...] = smoothed_twice(k)
            v.deep[...] = v.mmat[k]
        if k > SPLITS:
            v.ctot[...] += dot_nt(smoothed_twice(k).astype(bf16), v.deep[...])
            v.deep[...] = dot_nn(v.deep[...], v.mmat[k]).astype(bf16)
        if k == JOINED - 1:
            ld_i.wait()
            for item in handed_t:
                arrived(item)
            join_last()
        if k == LAST:
            v.deep_t[...] = jnp.transpose(v.deep[...].astype(f32)).astype(bf16)

    def join_last():
        for d in range(PIECES):
            cols = pl.ds(pl.multiple_of(lax.rem(j + d, PIECES) * ROWS, ROWS), ROWS)
            v.zpart[d] = dot_nt(v.last_t[d], v.cinv[:, cols])
        for d in range(PIECES):
            before, after = (d + PIECES - 1) % PIECES, (d + 1) % PIECES
            v.zmat[d, 0:64, :] = (v.zpart[d, 0:64, :] + v.zpart[before, 320:384, :]).astype(bf16)
            v.zmat[d, 64:192, :] = v.zpart[d, 64:192, :].astype(bf16)
            v.zmat[d, 192:256, :] = (v.zpart[d, 192:256, :] + v.zpart[after, 256:320, :]).astype(bf16)

    def to_pieces(ref, d):
        return remote(ref.at[0], ref.at[d], {"narrow": lax.rem(j + PIECES - d, PIECES)})

    handed_t = []
    last_t = []
    near = 1 + 2 * bits[0]
    half = pl.ds(pl.multiple_of(bits[0] * (WIDE // 2), WIDE // 2), WIDE // 2)
    shared = {}
    for k in range(JOINED):
        n, m = FIELDS[k], FIELDS[k + 1]
        bcat, pown, psend, precv, egive, ekeep, erecv = (
            v.__dict__[f"{x}{k}"] for x in ("bcat", "pown", "psend", "precv", "egive", "ekeep", "erecv")
        )
        keep, give = share(k)

        def product(rows):
            if k == 0:
                return v.first[rows, :] + dot_nn(bcat[rows, 256:384], v.tmat[0, 256:384, :])
            return dot_nn(bcat[rows, :], v.tmat[k])

        p = product(give)
        psend[...] = p[:, 0:ROWS].astype(bf16)
        low = lax.broadcasted_iota(jnp.int32, (m // 2, 128), 1) < BS

        def pack(ref, edge):
            top, rolled = edge[0:m // 2], pltpu.roll(edge[m // 2:], BS, 1)
            ref[0] = jnp.where(low, top, rolled).astype(bf16)
            ref[1] = jnp.where(low, rolled, top).astype(bf16)

        pack(egive, p[:, ROWS:])
        pieces = [
            remote(egive.at[0], erecv.at[2], {"wide": partners[k], "narrow": nxt}, has_next, has_prev),
            remote(egive.at[1], erecv.at[3], {"wide": partners[k], "narrow": prv}, has_prev, has_next),
            remote(psend, precv, {"wide": partners[k]}),
        ]
        edge = egive
        if m < n:
            p = product(keep)
            pack(ekeep, p[:, ROWS:])
            edge = ekeep
        pieces.append(remote(edge.at[0], erecv.at[0], {"narrow": nxt}, has_next, has_prev))
        pieces.append(remote(edge.at[1], erecv.at[1], {"narrow": prv}, has_prev, has_next))
        pown[...] = p[:, 0:ROWS]
        if k == 1:
            last_t.append(remote(v.last_t.at[0], v.last_t.at[near], {"narrow": lax.rem(j + PIECES - near, PIECES)}))
            last_t.append(remote(v.last_t.at[0, half], v.last_t.at[2, half], {"narrow": lax.rem(j + 2, PIECES)}))
        idle_work(k)
        if k == 2:
            for item in last_t:
                arrived(item)
            handed_t.append(remote(v.last_t.at[near], v.last_t.at[near], {"wide": partners[0]}))
            handed_t.append(remote(v.last_t.at[2, half], v.last_t.at[2, half], {"wide": partners[0]}))
        if k == SPLITS:
            for t in range(1, SPLITS):
                rows = own_rows(t)
                ref = v.__dict__[f"cfull{t}"]
                shared[t] = [
                    remote(ref.at[rows], ref.at[rows], {"wide": across(mask)}) for mask in range(1, 1 << t)
                ]
        for item in pieces:
            arrived(item)
        total = pown[...] + precv[...].astype(f32)
        after = v.__dict__[f"bcat{k + 1}"]
        v.__dict__[f"b32_{k + 1}"][...] = total
        after[:, 0:256] = total.astype(bf16)
        before = erecv[0].astype(f32) + erecv[2].astype(f32)
        behind = erecv[1].astype(f32) + erecv[3].astype(f32)
        after[0:m // 2, 256:384] = jnp.where(low, before, behind).astype(bf16)
        after[m // 2:, 256:384] = pltpu.roll(jnp.where(low, behind, before), BS, 1).astype(bf16)

    k = JOINED
    v.q_own[...] = dot_nn(v.bcat5[...], v.tmat[k, :, 0:256])
    v.q_all[0] = v.q_own[...].astype(bf16)
    gathers = [to_pieces(v.q_all, d) for d in (2, 1, 3)]
    far = remote(v.q_all.at[0], v.q_far, {"wide": partners[k]})
    idle_work(k)
    v.x_own[...] = dot_nn(v.q_all[0], v.zmat[0])
    for item in gathers:
        arrived(item)
    x = v.x_own[...]
    for d in (1, 2, 3):
        x = x + dot_nn(v.q_all[d], v.zmat[d])
    v.x_send[...] = x.astype(bf16)
    sums = [
        remote(v.x_send, v.x_recv.at[i], {"wide": across(mask << k)}) for i, mask in enumerate((2, 3, 1))
    ]
    v.x_own[...] = x
    arrived(far)
    v.b32_6[...] = v.q_own[...] + v.q_far[...].astype(f32)
    idle_work(LAST)

    b = v.b_std[...]
    dinv = jnp.concatenate([v.dcol[0]] * 4, axis=1)
    s = relax_down * b * dinv
    v.c_std[...] = s + relax_up * (b - dot_nn(v.a_cat[0, :, 0:256], s.astype(bf16))) * dinv
    v.fine[...] = v.mmat[0]
    for t in range(1, SPLITS):
        for item in shared[t]:
            arrived(item)
        v.c_std[...] += dot_nt(v.fine[...], v.__dict__[f"cfull{t}"][...])
        v.fine[...] = dot_nn(v.fine[...], v.mmat[t]).astype(bf16)
    for item in sums:
        arrived(item)
    x = v.x_own[...] + v.x_recv[0].astype(f32) + v.x_recv[1].astype(f32) + v.x_recv[2].astype(f32)
    x = v.ctot[...] + dot_nn(x.astype(bf16), v.deep_t[...])

    rows = own_rows(SPLITS)
    v.xg[rows, :] = x.astype(bf16)
    handed = [
        remote(v.xg.at[rows], v.xg.at[rows], {"wide": across(mask)}) for mask in reversed(mates)
    ]
    for item in handed:
        arrived(item)
    for c in range(4):
        cols = slice(c * 128, (c + 1) * 128)
        out[0, :, cols] = v.c_std[:, cols] + dot_nt(v.fine[...], v.xg[cols, :])
    for copy, sends in started:
        if sends is None:
            copy.wait_send()
        else:
            pl.when(sends)(copy.wait_send)


def on_device(rhs, gcol, galerkin, rcol, restrict, pcol, prolong, inverse):
    hbm = pl.BlockSpec(memory_space=pl.ANY)
    return pl.pallas_call(
        kernel,
        out_shape=pltpu.VMEM(rhs.shape, f32),
        in_specs=[hbm] * 8,
        out_specs=pl.BlockSpec(memory_space=pltpu.VMEM),
        scratch_shapes=list(scratch_specs().values()),
        compiler_params=pltpu.CompilerParams(
            collective_id=0, has_side_effects=True, vmem_limit_bytes=60 * 1024 * 1024
        ),
    )(
        jnp.transpose(gcol, (1, 3, 2, 0)),
        jnp.transpose(rcol, (1, 3, 2, 0)),
        jnp.transpose(pcol, (1, 2, 3, 0)),
        rhs, galerkin, restrict, prolong, inverse,
    )


def solution(mesh):
    in_specs = (
        P("wide", "narrow", None),
        P(None, "wide", "narrow", None),
        P(None, "wide", "narrow", None, None, None),
        P(None, "wide", "narrow", None),
        P(None, "wide", "narrow", None, None, None),
        P(None, "wide", "narrow", None),
        P(None, "wide", "narrow", None, None, None),
        P("narrow", None),
    )
    out_specs = P("wide", "narrow", None)
    return jax.shard_map(
        on_device, mesh=mesh, in_specs=in_specs, out_specs=out_specs, check_vma=False
    )
```

```python
import jax
import jax.numpy as jnp
from jax import lax
from jax.experimental import pallas as pl
from jax.experimental.pallas import tpu as pltpu
from jax.sharding import PartitionSpec as P

relax_down = 0.7
relax_up = 0.5

LEVELS = 7
SPLITS = 4
LAST = LEVELS - 1
JOINED = LEVELS - 2
BS = 64
NB = 4
ROWS = NB * BS
ALL = 512
PIECES = 4
WIDE = ROWS + 2 * BS
REMOTES = 96

f32 = jnp.float32
bf16 = jnp.bfloat16
NT = (((1,), (1,)), ((), ()))
FIELDS = [ALL >> min(level, SPLITS) for level in range(LEVELS + 1)]


def dot_nn(a, b):
    return jnp.dot(a, b, preferred_element_type=f32)


def dot_nt(a, b):
    return lax.dot_general(a, b, NT, preferred_element_type=f32)


def scratch_specs():
    vmem, dma = pltpu.VMEM, pltpu.SemaphoreType.DMA
    specs = {
        "gcol": pltpu.SMEM((1, 5, NB, LEVELS), jnp.int32),
        "rcol": pltpu.SMEM((1, 3, NB, LEVELS), jnp.int32),
        "pcol": pltpu.SMEM((1, NB, 2, LEVELS), jnp.int32),
        "b_std": vmem((ROWS, ALL), f32),
        "a_raw": vmem((LEVELS, NB, 5, BS, BS), bf16),
        "r_raw": vmem((LEVELS, NB, 3, BS, BS), bf16),
        "p_raw": vmem((LEVELS, NB, 2, BS, BS), bf16),
        "cinv": vmem((ROWS, PIECES * ROWS), bf16),
        "a_cat": vmem((LEVELS, ROWS, WIDE), bf16),
        "r_own": vmem((ROWS, ROWS), bf16),
        "p_own": vmem((ROWS, ROWS), bf16),
        "tmat": vmem((LEVELS, WIDE, WIDE), bf16),
        "mmat": vmem((LEVELS, ROWS, ROWS), bf16),
        "deep": vmem((ROWS, ROWS), bf16),
        "fine": vmem((ROWS, ROWS), bf16),
        "deep_t": vmem((ROWS, ROWS), bf16),
        "last_t": vmem((PIECES, WIDE, ROWS), bf16),
        "join_t": vmem((PIECES, WIDE, ROWS), bf16),
        "q_next": vmem((FIELDS[LEVELS], ROWS), bf16),
        "zpart": vmem((PIECES, WIDE, ROWS), f32),
        "zmat": vmem((PIECES, ROWS, ROWS), bf16),
        "drow": vmem((LEVELS, 8, ROWS), f32),
        "dcol": vmem((LEVELS, ROWS, 128), f32),
        "dsend": vmem((LEVELS, 8, 128), f32),
        "dhalo": vmem((2, LEVELS, 8, 128), f32),
        "edges": vmem((2 * BS, ALL), f32),
        "edge_diag": vmem((2, BS, BS), bf16),
        "h_send": vmem((2 * BS, ALL), bf16),
        "h_recv": vmem((2 * BS, ALL), bf16),
        "first": vmem((ALL, WIDE), f32),
        "ctot": vmem((FIELDS[LEVELS], ROWS), f32),
        "c_std": vmem((ROWS, ALL), f32),
        "q_all": vmem((PIECES, FIELDS[LEVELS], ROWS), bf16),
        "q_own": vmem((FIELDS[LEVELS], ROWS), f32),
        "q_far": vmem((FIELDS[LEVELS], ROWS), bf16),
        "x_own": vmem((FIELDS[LEVELS], ROWS), f32),
        "x_send": vmem((FIELDS[LEVELS], ROWS), bf16),
        "x_recv": vmem((7, FIELDS[LEVELS], ROWS), bf16),
        "xg": vmem((ALL, ROWS), bf16),
        "load_sem": dma((32,)),
        "send_sem": dma((REMOTES,)),
        "recv_sem": dma((REMOTES,)),
        "far_sem": pltpu.SemaphoreType.REGULAR((3, 2)),
    }
    for k in range(LEVELS):
        n, m = FIELDS[k], FIELDS[k + 1]
        if k > 0:
            specs[f"b32_{k}"] = vmem((n, ROWS), f32)
        if k < LAST:
            specs[f"bcat{k}"] = vmem((n, WIDE), bf16)
        if k < JOINED:
            specs[f"pown{k}"] = vmem((m, ROWS), f32)
            specs[f"psend{k}"] = vmem((m, ROWS), bf16)
            specs[f"precv{k}"] = vmem((m, ROWS), bf16)
            specs[f"egive{k}"] = vmem((2, m // 2, 128), bf16)
            specs[f"ekeep{k}"] = vmem((2, m // 2, 128), bf16)
            specs[f"erecv{k}"] = vmem((4, m // 2, 128), bf16)
        if 1 <= k < SPLITS:
            specs[f"cfull{k}"] = vmem((ALL, ROWS), bf16)
    return specs


class Refs:
    pass


def kernel(gcol_hbm, rcol_hbm, pcol_hbm, rhs_hbm, a_hbm, r_hbm, p_hbm, inv_hbm, out, *refs):
    v = Refs()
    for name, ref in zip(scratch_specs(), refs):
        setattr(v, name, ref)
    w = lax.axis_index("wide")
    j = lax.axis_index("narrow")
    nxt = lax.rem(j + 1, PIECES)
    prv = lax.rem(j + PIECES - 1, PIECES)
    has_next = j < PIECES - 1
    has_prev = j > 0
    bits = [lax.rem(w // (1 << k), 2) for k in range(LEVELS)]

    def across(mask):
        other = w
        for k in range(LEVELS):
            if mask >> k & 1:
                other = other + (1 - 2 * bits[k]) * (1 << k)
        return other

    partners = [across(1 << k) for k in range(LEVELS)]
    mates = range(1, 1 << SPLITS)

    def ring(distance):
        size = lax.axis_size("wide")
        return lax.rem(w + distance, size), lax.rem(w + size - distance, size)

    barrier = pltpu.get_barrier_semaphore()
    greeted = [{"narrow": lax.rem(j + d, PIECES)} for d in (1, 2, 3)]
    greeted += [{"wide": p} for p in partners[:3]]
    greeted += [{"wide": p} for p in ring(8)]
    for where in greeted:
        pl.semaphore_signal(barrier, inc=1, device_id=where)

    def pass_on(stage):
        up, down = ring(8 << stage)
        pl.semaphore_signal(v.far_sem.at[stage, 0], inc=1, device_id={"wide": up})
        pl.semaphore_signal(v.far_sem.at[stage, 1], inc=1, device_id={"wide": down})

    def passed(stage):
        pl.semaphore_wait(v.far_sem.at[stage, 0], 1)
        pl.semaphore_wait(v.far_sem.at[stage, 1], 1)

    n_load = [0]

    def load(src, dst):
        copy = pltpu.make_async_copy(src, dst, v.load_sem.at[n_load[0]])
        n_load[0] += 1
        copy.start()
        return copy

    ld_e = [
        load(a_hbm.at[0, 0, 3, 0], v.edge_diag.at[0]),
        load(a_hbm.at[0, 0, 0, 0], v.edge_diag.at[1]),
        load(rhs_hbm.at[0, 192:256], v.edges.at[0:64]),
        load(rhs_hbm.at[0, 0:64], v.edges.at[64:128]),
    ]
    ld_b = load(rhs_hbm.at[0], v.b_std)
    ld_g = load(gcol_hbm, v.gcol)
    ld_rc = load(rcol_hbm, v.rcol)
    ld_pc = load(pcol_hbm, v.pcol)
    ld_a0 = load(a_hbm.at[0, 0], v.a_raw.at[0])
    ld_r0 = load(r_hbm.at[0, 0], v.r_raw.at[0])
    rest = pl.ds(1, LEVELS - 1)
    ld_a = load(a_hbm.at[rest, 0], v.a_raw.at[rest])
    ld_r = load(r_hbm.at[rest, 0], v.r_raw.at[rest])
    ld_p = load(p_hbm.at[:, 0], v.p_raw)
    ld_i = load(inv_hbm, v.cinv)

    n_rem = [0]
    started = []

    def remote(src, dst, where, sends=None, recvs=None):
        idx = n_rem[0]
        n_rem[0] += 1
        copy = pltpu.make_async_remote_copy(
            src_ref=src, dst_ref=dst, send_sem=v.send_sem.at[idx], recv_sem=v.recv_sem.at[idx],
            device_id=where, device_id_type=pl.DeviceIdType.MESH,
        )
        if sends is None:
            copy.start()
        else:
            pl.when(sends)(copy.start)
        started.append((copy, sends))
        return copy, recvs

    def arrived(item):
        copy, recvs = item
        if recvs is None:
            copy.wait_recv()
        else:
            pl.when(recvs)(copy.wait_recv)

    def all_arrived(items):
        for copy, recvs in items:
            if recvs is None:
                copy.wait_recv()
        for side in (has_prev, has_next):
            def wait_side():
                for copy, recvs in items:
                    if recvs is side:
                        copy.wait_recv()

            pl.when(side)(wait_side)

    lane = lax.broadcasted_iota(jnp.int32, (BS, 2 * BS), 1)
    row = lax.broadcasted_iota(jnp.int32, (BS, 2 * BS), 0)
    upper = lane // BS
    on_low = row == lane
    on_high = row + BS == lane
    halo_code = jnp.where(upper == 0, jnp.where(has_prev, NB, -1), jnp.where(has_next, NB + 1, -1))

    def doubled(block):
        wide = block.astype(f32)
        return jnp.concatenate([wide, wide], axis=1)

    def pick(code, ids, blocks):
        total = jnp.where(code == ids[0], blocks[0], 0.0)
        for c, blk in zip(ids[1:], blocks[1:]):
            total = total + jnp.where(code == c, blk, 0.0)
        return total.astype(bf16)

    def each_block(body):
        def step(b, carry):
            body(b, pl.ds(pl.multiple_of(b * BS, BS), BS))
            return carry

        lax.fori_loop(0, NB, step, 0)

    def two_diagonals(k, low, high):
        picked = jnp.where(on_low, doubled(v.a_raw[k, low, 0]), 0.0)
        picked = picked + jnp.where(on_high, doubled(v.a_raw[k, high, 0]), 0.0)
        return 1.0 / jnp.sum(picked, axis=0, keepdims=True)

    def prep_diag(k):
        v.dsend[k] = jnp.broadcast_to(two_diagonals(k, 3, 0), (8, 128))
        v.drow[k, 0:1, 0:128] = two_diagonals(k, 0, 1)
        v.drow[k, 0:1, 128:256] = two_diagonals(k, 2, 3)

    def prep_t(k):
        def body(b, at):
            ids = [v.gcol[0, s, b, k] for s in range(5)]
            blocks = [doubled(v.a_raw[k, b, s]) for s in range(5)]
            v.a_cat[k, at, 0:128] = pick(upper, ids, blocks)
            v.a_cat[k, at, 128:256] = pick(upper + 2, ids, blocks)
            v.a_cat[k, at, 256:384] = pick(halo_code, ids, blocks)
            ids = [v.rcol[0, s, b, k] for s in range(3)]
            blocks = [doubled(v.r_raw[k, b, s]) for s in range(3)]
            v.r_own[at, 0:128] = pick(upper + NB * bits[k], ids, blocks)
            v.r_own[at, 128:256] = pick(upper + (2 + NB * bits[k]), ids, blocks)

        each_block(body)
        restrict = v.r_own[...]
        inner = dot_nn(restrict, v.a_cat[k])
        own = restrict.astype(f32) - relax_down * inner[:, 0:256] * v.drow[k, 0:1, :]
        outer = -relax_down * inner[:, 256:384]
        if k > 0:
            outer = outer * jnp.where(upper[0:1] == 0, v.dhalo[0, k, 0:1, :], v.dhalo[1, k, 0:1, :])
        for at, part in ((slice(0, 128), own[:, 0:128]), (slice(128, 256), own[:, 128:256]), (slice(256, 384), outer)):
            v.tmat[k, at, 0:256] = jnp.transpose(part).astype(bf16)
            ends = jnp.concatenate([part[192:256], part[0:64]], axis=0)
            v.tmat[k, at, 256:384] = jnp.transpose(ends).astype(bf16)

    def prep_m(k):
        def body(b, at):
            ids = [v.pcol[0, b, s, k] for s in range(2)]
            blocks = [doubled(v.p_raw[k, b, s]) for s in range(2)]
            v.p_own[at, 0:128] = pick(upper, ids, blocks)
            v.p_own[at, 128:256] = pick(upper + 2, ids, blocks)
            d = jnp.sum(jnp.where(on_low, doubled(v.a_raw[k, b, 0]), 0.0), axis=1, keepdims=True)
            v.dcol[k, at, :] = jnp.broadcast_to(1.0 / d, (BS, 128))

        each_block(body)
        prolong = v.p_own[...]
        inner = dot_nn(v.a_cat[k, :, 0:256], prolong)
        scale = jnp.concatenate([v.dcol[k], v.dcol[k]], axis=1)
        v.mmat[k] = (prolong.astype(f32) - relax_up * scale * inner).astype(bf16)

    def smoothed_twice(k):
        b = v.__dict__[f"b32_{k}"][...]
        dinv = v.drow[k, 0:1, :]
        s = relax_down * b * dinv
        return s + relax_up * (b - dot_nt(s.astype(bf16), v.a_cat[k, :, 0:256])) * dinv

    def share(k):
        n, m = FIELDS[k], FIELDS[k + 1]
        if m == n:
            return pl.ds(0, n), pl.ds(0, n)
        keep = pl.ds(pl.multiple_of(bits[k] * m, m), m)
        give = pl.ds(pl.multiple_of((1 - bits[k]) * m, m), m)
        return keep, give

    def own_rows(k):
        start = 0
        for t in range(min(k, SPLITS)):
            start = start + bits[t] * FIELDS[t + 1]
        return pl.ds(pl.multiple_of(start, FIELDS[k]), FIELDS[k]) if k else pl.ds(0, ALL)

    def no_halo(side):
        v.h_recv[side * BS:(side + 1) * BS, :] = jnp.zeros((BS, ALL), bf16)
        v.dhalo[side] = jnp.zeros((LEVELS, 8, 128), f32)
        for k in range(JOINED):
            ref = v.__dict__[f"erecv{k}"]
            zeros = jnp.zeros((FIELDS[k + 1] // 2, 128), bf16)
            ref[side] = zeros
            ref[2 + side] = zeros

    pl.when(j == 0)(lambda: no_halo(0))
    pl.when(j == PIECES - 1)(lambda: no_halo(1))

    for copy in ld_e:
        copy.wait()
    for i in range(2):
        at = slice(i * BS, (i + 1) * BS)
        d = jnp.sum(jnp.where(on_low, doubled(v.edge_diag[i]), 0.0), axis=1, keepdims=True)
        v.h_send[at, :] = (v.edges[at, :] * (1.0 / d)).astype(bf16)
    pl.semaphore_wait(barrier, len(greeted))
    halo = [
        remote(v.h_send.at[0:64], v.h_recv.at[0:64], {"narrow": nxt}, has_next, has_prev),
        remote(v.h_send.at[64:128], v.h_recv.at[64:128], {"narrow": prv}, has_prev, has_next),
    ]
    pass_on(0)
    ld_a0.wait()
    ld_a.wait()
    for k in range(LEVELS):
        prep_diag(k)
    diags = [
        remote(v.dsend, v.dhalo.at[0], {"narrow": nxt}, has_next, has_prev),
        remote(v.dsend, v.dhalo.at[1], {"narrow": prv}, has_prev, has_next),
    ]
    ld_b.wait()
    for c in range(4):
        cols = slice(c * 128, (c + 1) * 128)
        v.bcat0[cols, 0:256] = jnp.transpose(v.b_std[:, cols]).astype(bf16)
    ld_g.wait()
    ld_rc.wait()
    ld_r0.wait()
    prep_t(0)
    v.first[...] = dot_nn(v.bcat0[:, 0:256], v.tmat[0, 0:256, :])
    for item in halo:
        arrived(item)
    for c in range(4):
        cols = slice(c * 128, (c + 1) * 128)
        v.bcat0[cols, 256:384] = jnp.transpose(v.h_recv[:, cols].astype(f32)).astype(bf16)

    def idle_work(k):
        if k < 3:
            passed(k)
            if k < 2:
                pass_on(k + 1)
        if k == 0:
            ld_r.wait()
            for item in diags:
                arrived(item)
        if k == 0:
            prep_t(LAST)
            v.last_t[0] = v.tmat[LAST, :, 0:256]
            last_t.extend([fetch(v.last_t, True), fetch(v.last_t, False)])
        if k + 1 < JOINED:
            prep_t(k + 1)
        if k == 0:
            prep_t(JOINED)
            v.join_t[0] = v.tmat[JOINED, :, 0:256]
        if k == 0:
            ld_pc.wait()
            ld_p.wait()
        prep_m(k)
        if 1 <= k < SPLITS:
            c_bf = smoothed_twice(k).astype(bf16)
            v.__dict__[f"cfull{k}"][own_rows(k), :] = c_bf
        if k == SPLITS:
            v.ctot[...] = smoothed_twice(k)
            v.deep[...] = v.mmat[k]
        if k > SPLITS:
            v.ctot[...] += dot_nt(smoothed_twice(k).astype(bf16), v.deep[...])
            v.deep[...] = dot_nn(v.deep[...], v.mmat[k]).astype(bf16)
        if k == JOINED - 2:
            ld_i.wait()
            for item in handed_t:
                arrived(item)
            join(v.last_t, False)
        if k == JOINED - 1:
            for item in handed_j:
                arrived(item)
            join(v.join_t, True)
        if k == LAST:
            v.deep_t[...] = jnp.transpose(v.deep[...].astype(f32)).astype(bf16)

    def join(matrices, further):
        for d in range(PIECES):
            if further:
                v.zpart[d] = dot_nn(matrices[d], v.zmat[d])
                continue
            cols = pl.ds(pl.multiple_of(lax.rem(j + d, PIECES) * ROWS, ROWS), ROWS)
            v.zpart[d] = dot_nt(matrices[d], v.cinv[:, cols])
        for d in range(PIECES):
            before, after = (d + PIECES - 1) % PIECES, (d + 1) % PIECES
            v.zmat[d, 0:64, :] = (v.zpart[d, 0:64, :] + v.zpart[before, 320:384, :]).astype(bf16)
            v.zmat[d, 64:192, :] = v.zpart[d, 64:192, :].astype(bf16)
            v.zmat[d, 192:256, :] = (v.zpart[d, 192:256, :] + v.zpart[after, 256:320, :]).astype(bf16)

    def to_pieces(ref, d):
        return remote(ref.at[0], ref.at[d], {"narrow": lax.rem(j + PIECES - d, PIECES)})

    handed_t = []
    handed_j = []
    last_t = []
    join_t = []

    def fetch(ref, whole):
        if whole:
            return remote(ref.at[0], ref.at[near], {"narrow": lax.rem(j + PIECES - near, PIECES)})
        return remote(ref.at[0, half], ref.at[2, half], {"narrow": lax.rem(j + 2, PIECES)})

    def hand(ref, whole):
        part = ref.at[near] if whole else ref.at[2, half]
        return remote(part, part, {"wide": partners[0]})

    near = 1 + 2 * bits[0]
    half = pl.ds(pl.multiple_of(bits[0] * (WIDE // 2), WIDE // 2), WIDE // 2)
    shared = {}
    for k in range(JOINED):
        n, m = FIELDS[k], FIELDS[k + 1]
        bcat, pown, psend, precv, egive, ekeep, erecv = (
            v.__dict__[f"{x}{k}"] for x in ("bcat", "pown", "psend", "precv", "egive", "ekeep", "erecv")
        )
        keep, give = share(k)

        def product(rows):
            if k == 0:
                return v.first[rows, :] + dot_nn(bcat[rows, 256:384], v.tmat[0, 256:384, :])
            return dot_nn(bcat[rows, :], v.tmat[k])

        p = product(give)
        psend[...] = p[:, 0:ROWS].astype(bf16)
        if k == JOINED - 1:
            v.q_all[0] = psend[...]
            gathers = [to_pieces(v.q_all, d) for d in (2, 1, 3)]
        low = lax.broadcasted_iota(jnp.int32, (m // 2, 128), 1) < BS

        def pack(ref, edge):
            top, rolled = edge[0:m // 2], pltpu.roll(edge[m // 2:], BS, 1)
            ref[0] = jnp.where(low, top, rolled).astype(bf16)
            ref[1] = jnp.where(low, rolled, top).astype(bf16)

        pack(egive, p[:, ROWS:])
        pieces = [
            remote(egive.at[0], erecv.at[2], {"wide": partners[k], "narrow": nxt}, has_next, has_prev),
            remote(egive.at[1], erecv.at[3], {"wide": partners[k], "narrow": prv}, has_prev, has_next),
            remote(psend, precv, {"wide": partners[k]}),
        ]
        edge = egive
        if m < n:
            p = product(keep)
            pack(ekeep, p[:, ROWS:])
            edge = ekeep
        pieces.append(remote(edge.at[0], erecv.at[0], {"narrow": nxt}, has_next, has_prev))
        pieces.append(remote(edge.at[1], erecv.at[1], {"narrow": prv}, has_prev, has_next))
        pown[...] = p[:, 0:ROWS]
        if k == 1:
            join_t.append(fetch(v.join_t, True))
        if k == 3:
            join_t.append(fetch(v.join_t, False))
        if k == JOINED - 1:
            for item in join_t:
                arrived(item)
            handed_j += [hand(v.join_t, True), hand(v.join_t, False)]
        idle_work(k)
        if k == 2:
            for item in last_t:
                arrived(item)
            handed_t += [hand(v.last_t, True), hand(v.last_t, False)]
        if k == SPLITS:
            for t in range(1, SPLITS):
                rows = own_rows(t)
                ref = v.__dict__[f"cfull{t}"]
                shared[t] = [
                    remote(ref.at[rows], ref.at[rows], {"wide": across(mask)}) for mask in range(1, 1 << t)
                ]
        if k == JOINED - 1:
            v.x_own[...] = dot_nn(v.q_all[0], v.zmat[0])
            for item in gathers:
                arrived(item)
            x = v.x_own[...]
            for d in (1, 2, 3):
                x = x + dot_nn(v.q_all[d], v.zmat[d])
            v.x_send[...] = x.astype(bf16)
            sums = [
                remote(v.x_send, v.x_recv.at[i], {"wide": across(mask << k)})
                for i, mask in enumerate((4, 5, 3, 6, 2, 7, 1))
            ]
            v.x_own[...] = x
        all_arrived(pieces)
        total = pown[...] + precv[...].astype(f32)
        after = v.__dict__[f"bcat{k + 1}"]
        v.__dict__[f"b32_{k + 1}"][...] = total
        after[:, 0:256] = total.astype(bf16)
        before = erecv[0].astype(f32) + erecv[2].astype(f32)
        behind = erecv[1].astype(f32) + erecv[3].astype(f32)
        after[0:m // 2, 256:384] = jnp.where(low, before, behind).astype(bf16)
        after[m // 2:, 256:384] = pltpu.roll(jnp.where(low, behind, before), BS, 1).astype(bf16)

    k = JOINED
    v.q_own[...] = dot_nn(v.bcat5[...], v.tmat[k, :, 0:256])
    v.q_next[...] = v.q_own[...].astype(bf16)
    far = remote(v.q_next, v.q_far, {"wide": partners[k]})
    idle_work(k)

    b = v.b_std[...]
    dinv = jnp.concatenate([v.dcol[0]] * 4, axis=1)
    s = relax_down * b * dinv
    v.c_std[...] = s + relax_up * (b - dot_nn(v.a_cat[0, :, 0:256], s.astype(bf16))) * dinv
    v.fine[...] = v.mmat[0]
    for t in range(1, SPLITS):
        for item in shared[t]:
            arrived(item)
        v.c_std[...] += dot_nt(v.fine[...], v.__dict__[f"cfull{t}"][...])
        v.fine[...] = dot_nn(v.fine[...], v.mmat[t]).astype(bf16)
    arrived(far)
    v.b32_6[...] = v.q_own[...] + v.q_far[...].astype(f32)
    idle_work(LAST)
    for item in sums:
        arrived(item)
    x = v.x_own[...]
    for i in range(7):
        x = x + v.x_recv[i].astype(f32)
    x = v.ctot[...] + dot_nn(x.astype(bf16), v.deep_t[...])

    rows = own_rows(SPLITS)
    v.xg[rows, :] = x.astype(bf16)
    handed = [
        remote(v.xg.at[rows], v.xg.at[rows], {"wide": across(mask)}) for mask in reversed(mates)
    ]
    for item in handed:
        arrived(item)
    for c in range(4):
        cols = slice(c * 128, (c + 1) * 128)
        out[0, :, cols] = v.c_std[:, cols] + dot_nt(v.fine[...], v.xg[cols, :])
    for copy, sends in started:
        if sends is None:
            copy.wait_send()
        else:
            pl.when(sends)(copy.wait_send)


def on_device(rhs, gcol, galerkin, rcol, restrict, pcol, prolong, inverse):
    hbm = pl.BlockSpec(memory_space=pl.ANY)
    return pl.pallas_call(
        kernel,
        out_shape=pltpu.VMEM(rhs.shape, f32),
        in_specs=[hbm] * 8,
        out_specs=pl.BlockSpec(memory_space=pltpu.VMEM),
        scratch_shapes=list(scratch_specs().values()),
        compiler_params=pltpu.CompilerParams(
            collective_id=0, has_side_effects=True, vmem_limit_bytes=60 * 1024 * 1024
        ),
    )(
        jnp.transpose(gcol, (1, 3, 2, 0)),
        jnp.transpose(rcol, (1, 3, 2, 0)),
        jnp.transpose(pcol, (1, 2, 3, 0)),
        rhs, galerkin, restrict, prolong, inverse,
    )


def solution(mesh):
    in_specs = (
        P("wide", "narrow", None),
        P(None, "wide", "narrow", None),
        P(None, "wide", "narrow", None, None, None),
        P(None, "wide", "narrow", None),
        P(None, "wide", "narrow", None, None, None),
        P(None, "wide", "narrow", None),
        P(None, "wide", "narrow", None, None, None),
        P("narrow", None),
    )
    out_specs = P("wide", "narrow", None)
    return jax.shard_map(
        on_device, mesh=mesh, in_specs=in_specs, out_specs=out_specs, check_vma=False
    )
```

```python
import jax
import jax.numpy as jnp
from jax import lax
from jax.experimental import pallas as pl
from jax.experimental.pallas import tpu as pltpu
from jax.sharding import PartitionSpec as P

relax_down = 0.7
relax_up = 0.5

LEVELS = 7
SPLITS = 4
LAST = LEVELS - 1
JOINED = LEVELS - 2
BS = 64
NB = 4
ROWS = NB * BS
ALL = 512
PIECES = 4
WIDE = ROWS + 2 * BS
REMOTES = 96

f32 = jnp.float32
bf16 = jnp.bfloat16
NT = (((1,), (1,)), ((), ()))
FIELDS = [ALL >> min(level, SPLITS) for level in range(LEVELS + 1)]


def dot_nn(a, b):
    return jnp.dot(a, b, preferred_element_type=f32)


def dot_nt(a, b):
    return lax.dot_general(a, b, NT, preferred_element_type=f32)


def scratch_specs():
    vmem, dma = pltpu.VMEM, pltpu.SemaphoreType.DMA
    specs = {
        "gcol": pltpu.SMEM((1, 5, NB, LEVELS), jnp.int32),
        "rcol": pltpu.SMEM((1, 3, NB, LEVELS), jnp.int32),
        "pcol": pltpu.SMEM((1, NB, 2, LEVELS), jnp.int32),
        "b_std": vmem((ROWS, ALL), f32),
        "a_raw": vmem((LEVELS, NB, 5, BS, BS), bf16),
        "r_raw": vmem((LEVELS, NB, 3, BS, BS), bf16),
        "p_raw": vmem((LEVELS, NB, 2, BS, BS), bf16),
        "cinv": vmem((ROWS, PIECES * ROWS), bf16),
        "a_cat": vmem((LEVELS, ROWS, WIDE), bf16),
        "r_own": vmem((ROWS, ROWS), bf16),
        "p_own": vmem((ROWS, ROWS), bf16),
        "tmat": vmem((LEVELS, WIDE, WIDE), bf16),
        "mmat": vmem((LEVELS, ROWS, ROWS), bf16),
        "deep": vmem((ROWS, ROWS), bf16),
        "fine": vmem((ROWS, ROWS), bf16),
        "deep_t": vmem((ROWS, ROWS), bf16),
        "last_t": vmem((PIECES, WIDE, ROWS), bf16),
        "join_t": vmem((PIECES, WIDE, ROWS), bf16),
        "q_next": vmem((FIELDS[LEVELS], ROWS), bf16),
        "zpart": vmem((PIECES, WIDE, ROWS), f32),
        "zmat": vmem((PIECES, ROWS, ROWS), bf16),
        "drow": vmem((LEVELS, 8, ROWS), f32),
        "dcol": vmem((LEVELS, ROWS, 128), f32),
        "dsend": vmem((LEVELS, 8, 128), f32),
        "dhalo": vmem((2, LEVELS, 8, 128), f32),
        "edges": vmem((2 * BS, ALL), f32),
        "edge_diag": vmem((2, BS, BS), bf16),
        "h_send": vmem((2 * BS, ALL), bf16),
        "h_recv": vmem((2 * BS, ALL), bf16),
        "first": vmem((ALL, WIDE), f32),
        "ctot": vmem((FIELDS[LEVELS], ROWS), f32),
        "c_std": vmem((ROWS, ALL), f32),
        "q_all": vmem((PIECES, FIELDS[LEVELS], ROWS), bf16),
        "q_own": vmem((FIELDS[LEVELS], ROWS), f32),
        "q_far": vmem((FIELDS[LEVELS], ROWS), bf16),
        "x_own": vmem((FIELDS[LEVELS], ROWS), f32),
        "x_send": vmem((FIELDS[LEVELS], ROWS), bf16),
        "x_recv": vmem((7, FIELDS[LEVELS], ROWS), bf16),
        "xg": vmem((ALL, ROWS), bf16),
        "load_sem": dma((32,)),
        "send_sem": dma((REMOTES,)),
        "recv_sem": dma((REMOTES,)),
        "far_sem": pltpu.SemaphoreType.REGULAR((3, 2)),
    }
    for k in range(LEVELS):
        n, m = FIELDS[k], FIELDS[k + 1]
        if k > 0:
            specs[f"b32_{k}"] = vmem((n, ROWS), f32)
        if k < LAST:
            specs[f"bcat{k}"] = vmem((n, WIDE), bf16)
        if k < JOINED:
            specs[f"pown{k}"] = vmem((m, ROWS), f32)
            specs[f"psend{k}"] = vmem((m, ROWS), bf16)
            specs[f"precv{k}"] = vmem((m, ROWS), bf16)
            specs[f"egive{k}"] = vmem((2, m // 2, 128), bf16)
            specs[f"ekeep{k}"] = vmem((2, m // 2, 128), bf16)
            specs[f"erecv{k}"] = vmem((4, m // 2, 128), bf16)
        if 1 <= k < SPLITS:
            specs[f"cfull{k}"] = vmem((ALL, ROWS), bf16)
    return specs


class Refs:
    pass


def kernel(gcol_hbm, rcol_hbm, pcol_hbm, rhs_hbm, a_hbm, r_hbm, p_hbm, inv_hbm, out, *refs):
    v = Refs()
    for name, ref in zip(scratch_specs(), refs):
        setattr(v, name, ref)
    w = lax.axis_index("wide")
    j = lax.axis_index("narrow")
    nxt = lax.rem(j + 1, PIECES)
    prv = lax.rem(j + PIECES - 1, PIECES)
    has_next = j < PIECES - 1
    has_prev = j > 0
    bits = [lax.rem(w // (1 << k), 2) for k in range(LEVELS)]

    def across(mask):
        other = w
        for k in range(LEVELS):
            if mask >> k & 1:
                other = other + (1 - 2 * bits[k]) * (1 << k)
        return other

    partners = [across(1 << k) for k in range(LEVELS)]
    mates = range(1, 1 << SPLITS)

    def ring(distance):
        size = lax.axis_size("wide")
        return lax.rem(w + distance, size), lax.rem(w + size - distance, size)

    barrier = pltpu.get_barrier_semaphore()
    y = lax.rem(w // 2, 4)
    greeted = [{"narrow": nxt}, {"narrow": prv}, {"wide": partners[0]}]
    greeted += [{"wide": w + 2 * (lax.rem(y + d, 4) - y)} for d in (1, 3)]
    greeted += [{"wide": p} for p in ring(8)]
    for where in greeted:
        pl.semaphore_signal(barrier, inc=1, device_id=where)

    def pass_on(stage):
        up, down = ring(8 << stage)
        pl.semaphore_signal(v.far_sem.at[stage, 0], inc=1, device_id={"wide": up})
        pl.semaphore_signal(v.far_sem.at[stage, 1], inc=1, device_id={"wide": down})

    def passed(stage):
        pl.semaphore_wait(v.far_sem.at[stage, 0], 1)
        pl.semaphore_wait(v.far_sem.at[stage, 1], 1)

    n_load = [0]

    def load(src, dst):
        copy = pltpu.make_async_copy(src, dst, v.load_sem.at[n_load[0]])
        n_load[0] += 1
        copy.start()
        return copy

    ld_e = [
        load(a_hbm.at[0, 0, 3, 0], v.edge_diag.at[0]),
        load(a_hbm.at[0, 0, 0, 0], v.edge_diag.at[1]),
        load(rhs_hbm.at[0, 192:256], v.edges.at[0:64]),
        load(rhs_hbm.at[0, 0:64], v.edges.at[64:128]),
    ]
    ld_b = load(rhs_hbm.at[0], v.b_std)
    ld_g = load(gcol_hbm, v.gcol)
    ld_rc = load(rcol_hbm, v.rcol)
    ld_pc = load(pcol_hbm, v.pcol)
    ld_a0 = load(a_hbm.at[0, 0], v.a_raw.at[0])
    ld_r0 = load(r_hbm.at[0, 0], v.r_raw.at[0])
    rest = pl.ds(1, LEVELS - 1)
    ld_a = load(a_hbm.at[rest, 0], v.a_raw.at[rest])
    ld_r = load(r_hbm.at[rest, 0], v.r_raw.at[rest])
    ld_p = load(p_hbm.at[:, 0], v.p_raw)
    ld_i = load(inv_hbm, v.cinv)

    n_rem = [0]
    started = []

    def remote(src, dst, where, sends=None, recvs=None):
        idx = n_rem[0]
        n_rem[0] += 1
        copy = pltpu.make_async_remote_copy(
            src_ref=src, dst_ref=dst, send_sem=v.send_sem.at[idx], recv_sem=v.recv_sem.at[idx],
            device_id=where, device_id_type=pl.DeviceIdType.MESH,
        )
        if sends is None:
            copy.start()
        else:
            pl.when(sends)(copy.start)
        started.append((copy, sends))
        return copy, recvs

    def arrived(item):
        copy, recvs = item
        if recvs is None:
            copy.wait_recv()
        else:
            pl.when(recvs)(copy.wait_recv)

    def all_arrived(items):
        for copy, recvs in items:
            if recvs is None:
                copy.wait_recv()
        for side in (has_prev, has_next):
            def wait_side():
                for copy, recvs in items:
                    if recvs is side:
                        copy.wait_recv()

            pl.when(side)(wait_side)

    lane = lax.broadcasted_iota(jnp.int32, (BS, 2 * BS), 1)
    row = lax.broadcasted_iota(jnp.int32, (BS, 2 * BS), 0)
    upper = lane // BS
    on_low = row == lane
    on_high = row + BS == lane
    halo_code = jnp.where(upper == 0, jnp.where(has_prev, NB, -1), jnp.where(has_next, NB + 1, -1))

    def doubled(block):
        wide = block.astype(f32)
        return jnp.concatenate([wide, wide], axis=1)

    def pick(code, ids, blocks):
        total = jnp.where(code == ids[0], blocks[0], 0.0)
        for c, blk in zip(ids[1:], blocks[1:]):
            total = total + jnp.where(code == c, blk, 0.0)
        return total.astype(bf16)

    def each_block(body):
        def step(b, carry):
            body(b, pl.ds(pl.multiple_of(b * BS, BS), BS))
            return carry

        lax.fori_loop(0, NB, step, 0)

    def two_diagonals(k, low, high):
        picked = jnp.where(on_low, doubled(v.a_raw[k, low, 0]), 0.0)
        picked = picked + jnp.where(on_high, doubled(v.a_raw[k, high, 0]), 0.0)
        return 1.0 / jnp.sum(picked, axis=0, keepdims=True)

    def prep_diag(k):
        v.dsend[k] = jnp.broadcast_to(two_diagonals(k, 3, 0), (8, 128))
        v.drow[k, 0:1, 0:128] = two_diagonals(k, 0, 1)
        v.drow[k, 0:1, 128:256] = two_diagonals(k, 2, 3)

    def prep_t(k):
        def body(b, at):
            ids = [v.gcol[0, s, b, k] for s in range(5)]
            blocks = [doubled(v.a_raw[k, b, s]) for s in range(5)]
            v.a_cat[k, at, 0:128] = pick(upper, ids, blocks)
            v.a_cat[k, at, 128:256] = pick(upper + 2, ids, blocks)
            v.a_cat[k, at, 256:384] = pick(halo_code, ids, blocks)
            ids = [v.rcol[0, s, b, k] for s in range(3)]
            blocks = [doubled(v.r_raw[k, b, s]) for s in range(3)]
            v.r_own[at, 0:128] = pick(upper + NB * bits[k], ids, blocks)
            v.r_own[at, 128:256] = pick(upper + (2 + NB * bits[k]), ids, blocks)

        each_block(body)
        restrict = v.r_own[...]
        inner = dot_nn(restrict, v.a_cat[k])
        own = restrict.astype(f32) - relax_down * inner[:, 0:256] * v.drow[k, 0:1, :]
        outer = -relax_down * inner[:, 256:384]
        if k > 0:
            outer = outer * jnp.where(upper[0:1] == 0, v.dhalo[0, k, 0:1, :], v.dhalo[1, k, 0:1, :])
        for at, part in ((slice(0, 128), own[:, 0:128]), (slice(128, 256), own[:, 128:256]), (slice(256, 384), outer)):
            v.tmat[k, at, 0:256] = jnp.transpose(part).astype(bf16)
            ends = jnp.concatenate([part[192:256], part[0:64]], axis=0)
            v.tmat[k, at, 256:384] = jnp.transpose(ends).astype(bf16)

    def prep_m(k):
        def body(b, at):
            ids = [v.pcol[0, b, s, k] for s in range(2)]
            blocks = [doubled(v.p_raw[k, b, s]) for s in range(2)]
            v.p_own[at, 0:128] = pick(upper, ids, blocks)
            v.p_own[at, 128:256] = pick(upper + 2, ids, blocks)
            d = jnp.sum(jnp.where(on_low, doubled(v.a_raw[k, b, 0]), 0.0), axis=1, keepdims=True)
            v.dcol[k, at, :] = jnp.broadcast_to(1.0 / d, (BS, 128))

        each_block(body)
        prolong = v.p_own[...]
        inner = dot_nn(v.a_cat[k, :, 0:256], prolong)
        scale = jnp.concatenate([v.dcol[k], v.dcol[k]], axis=1)
        v.mmat[k] = (prolong.astype(f32) - relax_up * scale * inner).astype(bf16)

    def smoothed_twice(k):
        b = v.__dict__[f"b32_{k}"][...]
        dinv = v.drow[k, 0:1, :]
        s = relax_down * b * dinv
        return s + relax_up * (b - dot_nt(s.astype(bf16), v.a_cat[k, :, 0:256])) * dinv

    def share(k):
        n, m = FIELDS[k], FIELDS[k + 1]
        if m == n:
            return pl.ds(0, n), pl.ds(0, n)
        keep = pl.ds(pl.multiple_of(bits[k] * m, m), m)
        give = pl.ds(pl.multiple_of((1 - bits[k]) * m, m), m)
        return keep, give

    def own_rows(k):
        start = 0
        for t in range(min(k, SPLITS)):
            start = start + bits[t] * FIELDS[t + 1]
        return pl.ds(pl.multiple_of(start, FIELDS[k]), FIELDS[k]) if k else pl.ds(0, ALL)

    def no_halo(side):
        v.h_recv[side * BS:(side + 1) * BS, :] = jnp.zeros((BS, ALL), bf16)
        v.dhalo[side] = jnp.zeros((LEVELS, 8, 128), f32)
        for k in range(JOINED):
            ref = v.__dict__[f"erecv{k}"]
            zeros = jnp.zeros((FIELDS[k + 1] // 2, 128), bf16)
            ref[side] = zeros
            ref[2 + side] = zeros

    pl.when(j == 0)(lambda: no_halo(0))
    pl.when(j == PIECES - 1)(lambda: no_halo(1))

    for copy in ld_e:
        copy.wait()
    for i in range(2):
        at = slice(i * BS, (i + 1) * BS)
        d = jnp.sum(jnp.where(on_low, doubled(v.edge_diag[i]), 0.0), axis=1, keepdims=True)
        v.h_send[at, :] = (v.edges[at, :] * (1.0 / d)).astype(bf16)
    pl.semaphore_wait(barrier, len(greeted))
    halo = [
        remote(v.h_send.at[0:64], v.h_recv.at[0:64], {"narrow": nxt}, has_next, has_prev),
        remote(v.h_send.at[64:128], v.h_recv.at[64:128], {"narrow": prv}, has_prev, has_next),
    ]
    pass_on(0)
    ld_a0.wait()
    ld_a.wait()
    for k in range(LEVELS):
        prep_diag(k)
    diags = [
        remote(v.dsend, v.dhalo.at[0], {"narrow": nxt}, has_next, has_prev),
        remote(v.dsend, v.dhalo.at[1], {"narrow": prv}, has_prev, has_next),
    ]
    ld_b.wait()
    for c in range(4):
        cols = slice(c * 128, (c + 1) * 128)
        v.bcat0[cols, 0:256] = jnp.transpose(v.b_std[:, cols]).astype(bf16)
    ld_g.wait()
    ld_rc.wait()
    ld_r0.wait()
    prep_t(0)
    v.first[...] = dot_nn(v.bcat0[:, 0:256], v.tmat[0, 0:256, :])
    for item in halo:
        arrived(item)
    for c in range(4):
        cols = slice(c * 128, (c + 1) * 128)
        v.bcat0[cols, 256:384] = jnp.transpose(v.h_recv[:, cols].astype(f32)).astype(bf16)

    def idle_work(k):
        if k < 3:
            passed(k)
            if k < 2:
                pass_on(k + 1)
        if k == 0:
            ld_r.wait()
            for item in diags:
                arrived(item)
        if k == 0:
            prep_t(LAST)
            v.last_t[0] = v.tmat[LAST, :, 0:256]
            last_t.extend([fetch(v.last_t, True), fetch(v.last_t, False)])
        if k + 1 < JOINED:
            prep_t(k + 1)
        if k == 0:
            prep_t(JOINED)
            v.join_t[0] = v.tmat[JOINED, :, 0:256]
        if k == 0:
            ld_pc.wait()
            ld_p.wait()
        prep_m(k)
        if 1 <= k < SPLITS:
            c_bf = smoothed_twice(k).astype(bf16)
            v.__dict__[f"cfull{k}"][own_rows(k), :] = c_bf
        if k == SPLITS:
            v.ctot[...] = smoothed_twice(k)
            v.deep[...] = v.mmat[k]
        if k > SPLITS:
            v.ctot[...] += dot_nt(smoothed_twice(k).astype(bf16), v.deep[...])
            v.deep[...] = dot_nn(v.deep[...], v.mmat[k]).astype(bf16)
        if k == JOINED - 2:
            ld_i.wait()
            for item in handed_t:
                arrived(item)
            join(v.last_t, False)
        if k == JOINED - 1:
            for item in handed_j:
                arrived(item)
            join(v.join_t, True)
        if k == LAST:
            v.deep_t[...] = jnp.transpose(v.deep[...].astype(f32)).astype(bf16)

    def join(matrices, further):
        for d in range(PIECES):
            if further:
                v.zpart[d] = dot_nn(matrices[d], v.zmat[d])
                continue
            cols = pl.ds(pl.multiple_of(lax.rem(j + d, PIECES) * ROWS, ROWS), ROWS)
            v.zpart[d] = dot_nt(matrices[d], v.cinv[:, cols])
        for d in range(PIECES):
            before, after = (d + PIECES - 1) % PIECES, (d + 1) % PIECES
            v.zmat[d, 0:64, :] = (v.zpart[d, 0:64, :] + v.zpart[before, 320:384, :]).astype(bf16)
            v.zmat[d, 64:192, :] = v.zpart[d, 64:192, :].astype(bf16)
            v.zmat[d, 192:256, :] = (v.zpart[d, 192:256, :] + v.zpart[after, 256:320, :]).astype(bf16)

    def to_pieces(ref, d):
        return remote(ref.at[0], ref.at[d], {"narrow": lax.rem(j + PIECES - d, PIECES)})

    handed_t = []
    handed_j = []
    last_t = []
    join_t = []

    def fetch(ref, whole):
        if whole:
            return remote(ref.at[0], ref.at[near], {"narrow": lax.rem(j + PIECES - near, PIECES)})
        return remote(ref.at[0, half], ref.at[2, half], {"narrow": lax.rem(j + 2, PIECES)})

    def hand(ref, whole):
        part = ref.at[near] if whole else ref.at[2, half]
        return remote(part, part, {"wide": partners[0]})

    near = 1 + 2 * bits[0]
    half = pl.ds(pl.multiple_of(bits[0] * (WIDE // 2), WIDE // 2), WIDE // 2)
    shared = {}
    for k in range(JOINED):
        n, m = FIELDS[k], FIELDS[k + 1]
        bcat, pown, psend, precv, egive, ekeep, erecv = (
            v.__dict__[f"{x}{k}"] for x in ("bcat", "pown", "psend", "precv", "egive", "ekeep", "erecv")
        )
        keep, give = share(k)

        def product(rows):
            if k == 0:
                return v.first[rows, :] + dot_nn(bcat[rows, 256:384], v.tmat[0, 256:384, :])
            return dot_nn(bcat[rows, :], v.tmat[k])

        p = product(give)
        psend[...] = p[:, 0:ROWS].astype(bf16)
        if k == JOINED - 1:
            v.q_all[0] = psend[...]
            gathers = [to_pieces(v.q_all, d) for d in (2, 1, 3)]
        low = lax.broadcasted_iota(jnp.int32, (m // 2, 128), 1) < BS

        def pack(ref, edge):
            top, rolled = edge[0:m // 2], pltpu.roll(edge[m // 2:], BS, 1)
            ref[0] = jnp.where(low, top, rolled).astype(bf16)
            ref[1] = jnp.where(low, rolled, top).astype(bf16)

        pack(egive, p[:, ROWS:])
        pieces = [
            remote(egive.at[0], erecv.at[2], {"wide": partners[k], "narrow": nxt}, has_next, has_prev),
            remote(egive.at[1], erecv.at[3], {"wide": partners[k], "narrow": prv}, has_prev, has_next),
            remote(psend, precv, {"wide": partners[k]}),
        ]
        edge = egive
        if m < n:
            p = product(keep)
            pack(ekeep, p[:, ROWS:])
            edge = ekeep
        pieces.append(remote(edge.at[0], erecv.at[0], {"narrow": nxt}, has_next, has_prev))
        pieces.append(remote(edge.at[1], erecv.at[1], {"narrow": prv}, has_prev, has_next))
        pown[...] = p[:, 0:ROWS]
        if k == 1:
            join_t.append(fetch(v.join_t, True))
        if k == 3:
            join_t.append(fetch(v.join_t, False))
        if k == JOINED - 1:
            for item in join_t:
                arrived(item)
            handed_j += [hand(v.join_t, True), hand(v.join_t, False)]
        idle_work(k)
        if k == 2:
            for item in last_t:
                arrived(item)
            handed_t += [hand(v.last_t, True), hand(v.last_t, False)]
        if k == SPLITS:
            for t in range(1, SPLITS):
                rows = own_rows(t)
                ref = v.__dict__[f"cfull{t}"]
                shared[t] = [
                    remote(ref.at[rows], ref.at[rows], {"wide": across(mask)}) for mask in range(1, 1 << t)
                ]
        if k == JOINED - 1:
            v.x_own[...] = dot_nn(v.q_all[0], v.zmat[0])
            for item in gathers:
                arrived(item)
            x = v.x_own[...]
            for d in (1, 2, 3):
                x = x + dot_nn(v.q_all[d], v.zmat[d])
            v.x_send[...] = x.astype(bf16)
            sums = [
                remote(v.x_send, v.x_recv.at[i], {"wide": across(mask << k)})
                for i, mask in enumerate((4, 5, 3, 6, 2, 7, 1))
            ]
            v.x_own[...] = x
        all_arrived(pieces)
        total = pown[...] + precv[...].astype(f32)
        after = v.__dict__[f"bcat{k + 1}"]
        v.__dict__[f"b32_{k + 1}"][...] = total
        after[:, 0:256] = total.astype(bf16)
        before = erecv[0].astype(f32) + erecv[2].astype(f32)
        behind = erecv[1].astype(f32) + erecv[3].astype(f32)
        after[0:m // 2, 256:384] = jnp.where(low, before, behind).astype(bf16)
        after[m // 2:, 256:384] = pltpu.roll(jnp.where(low, behind, before), BS, 1).astype(bf16)

    k = JOINED
    v.q_own[...] = dot_nn(v.bcat5[...], v.tmat[k, :, 0:256])
    v.q_next[...] = v.q_own[...].astype(bf16)
    far = remote(v.q_next, v.q_far, {"wide": partners[k]})
    idle_work(k)

    b = v.b_std[...]
    dinv = jnp.concatenate([v.dcol[0]] * 4, axis=1)
    s = relax_down * b * dinv
    v.c_std[...] = s + relax_up * (b - dot_nn(v.a_cat[0, :, 0:256], s.astype(bf16))) * dinv
    v.fine[...] = v.mmat[0]
    for t in range(1, SPLITS):
        for item in shared[t]:
            arrived(item)
        v.c_std[...] += dot_nt(v.fine[...], v.__dict__[f"cfull{t}"][...])
        v.fine[...] = dot_nn(v.fine[...], v.mmat[t]).astype(bf16)
    arrived(far)
    v.b32_6[...] = v.q_own[...] + v.q_far[...].astype(f32)
    idle_work(LAST)
    for item in sums:
        arrived(item)
    x = v.x_own[...]
    for i in range(7):
        x = x + v.x_recv[i].astype(f32)
    x = v.ctot[...] + dot_nn(x.astype(bf16), v.deep_t[...])

    rows = own_rows(SPLITS)
    v.xg[rows, :] = x.astype(bf16)
    handed = [
        remote(v.xg.at[rows], v.xg.at[rows], {"wide": across(mask)}) for mask in reversed(mates)
    ]
    for item in handed:
        arrived(item)
    for c in range(4):
        cols = slice(c * 128, (c + 1) * 128)
        out[0, :, cols] = v.c_std[:, cols] + dot_nt(v.fine[...], v.xg[cols, :])
    for copy, sends in started:
        if sends is None:
            copy.wait_send()
        else:
            pl.when(sends)(copy.wait_send)


def on_device(rhs, gcol, galerkin, rcol, restrict, pcol, prolong, inverse):
    hbm = pl.BlockSpec(memory_space=pl.ANY)
    return pl.pallas_call(
        kernel,
        out_shape=pltpu.VMEM(rhs.shape, f32),
        in_specs=[hbm] * 8,
        out_specs=pl.BlockSpec(memory_space=pltpu.VMEM),
        scratch_shapes=list(scratch_specs().values()),
        compiler_params=pltpu.CompilerParams(
            collective_id=0, has_side_effects=True, vmem_limit_bytes=60 * 1024 * 1024
        ),
    )(
        jnp.transpose(gcol, (1, 3, 2, 0)),
        jnp.transpose(rcol, (1, 3, 2, 0)),
        jnp.transpose(pcol, (1, 2, 3, 0)),
        rhs, galerkin, restrict, prolong, inverse,
    )


def solution(mesh):
    in_specs = (
        P("wide", "narrow", None),
        P(None, "wide", "narrow", None),
        P(None, "wide", "narrow", None, None, None),
        P(None, "wide", "narrow", None),
        P(None, "wide", "narrow", None, None, None),
        P(None, "wide", "narrow", None),
        P(None, "wide", "narrow", None, None, None),
        P("narrow", None),
    )
    out_specs = P("wide", "narrow", None)
    return jax.shard_map(
        on_device, mesh=mesh, in_specs=in_specs, out_specs=out_specs, check_vma=False
    )
```
